32 devices in a mesh: tgt: 2 (over core), sup: 16 (over z, y, x).
Axes of the slice: x: 2, y: 2, z: 4, core: 2. Of those that a mesh axis runs over, the one named last changes fastest.
Arguments:
- image_pool: bfloat16 [2048, 3072], P(('tgt', 'sup')), may hold values from -1 to 2
- target_index: int32 [64], replicated, may hold values from 0 to 2047, as said below
- labels: int32 [64], P('tgt'), may hold values from 0 to 1023
- support: float32 [64, 3, 1024], P('sup'), may hold values from -1 to 2
- ridge_coef: float32 [64, 1024], P('sup'), may hold values from -1.5 to 1.5
Outputs:
- residual: float32 [64, 1024], P('tgt', 'sup')
- support_grad: float32 [64, 3, 1024], P('sup')
The draws below stay inside these ranges and needn't reach their ends.
Inputs may be any that keep to these rules, and one draw needn't show every extreme that they name: `target_index`: any row of the pool; the first of each group's 32 targets lies in the pool rows of the devices half the tgt axis away.
All inputs are finite; a program needn't handle non-finite values.
Results may differ from the reference program's by a relative error of at most 0.0003.
Values may be sent and summed in bfloat16 or wider, within the bound.
A program may use at most 64 MiB of HBM per device.

```python
import math
import jax
import jax.numpy as jnp
from jax import lax

SIDE = 32
CHAN = 3
CLASSES = 1024
LAYERS = 4
TGT_DEV = 32
PIX = 1024
TARGETS = 64
SUPPORTS = 64
POOL = 2048
N_TGT = 2


def draw_target_index(key, part):
    groups = TARGETS // TGT_DEV
    span = POOL // groups
    position = jnp.arange(TARGETS, dtype=jnp.int32)
    group = position // TGT_DEV
    anywhere = jax.random.randint(jax.random.fold_in(key, 17), (TARGETS,), 0, POOL, dtype=jnp.int32)
    offset = jax.random.randint(jax.random.fold_in(key, 29), (TARGETS,), 0, span, dtype=jnp.int32)
    far_group = (group + groups // 2) % groups
    far_row = far_group * span + offset
    rows = jnp.where(position % TGT_DEV == 0, far_row, anywhere)
    rows = jnp.where(position == 1, 0, rows)
    rows = jnp.where(position == TARGETS - 1, POOL - 1, rows)
    return rows.astype(jnp.int32)


def plant(values, stream_key, low, high):
    longest = values.shape.index(max(values.shape))
    spots = []
    for shift in (0, 1):
        where = [jax.random.randint(jax.random.fold_in(stream_key, axis), (), 0, length) for axis, length in enumerate(values.shape)]
        where[longest] = (where[longest] + shift) % values.shape[longest]
        spots.append(tuple(where))
    return values.at[spots[0]].set(low).at[spots[1]].set(high)


def block_scale(key, dims, pieces, smallest, top_value):
    def one(axis_at, parts):
        steps = jax.random.uniform(jax.random.fold_in(jax.random.fold_in(key, 6), axis_at), (parts,), jnp.float32, smallest / len(pieces), top_value / len(pieces))
        return jnp.repeat(jnp.exp(steps), dims[axis_at] // parts).reshape((-1,) + (1,) * (len(dims) - axis_at - 1))

    loudness = one(*pieces[0])
    for cut in pieces[1:]:
        loudness = loudness * one(*cut)
    return loudness


def bell_draw(key, shape, width, reach, cuts=(), held_as=jnp.bfloat16):
    array = jax.random.normal(key, shape, jnp.float32) * width
    if len(cuts) > 0:
        array = block_scale(key, shape, cuts, -0.22, 0.18) * array
    return jnp.clip(array, min=-reach, max=reach).astype(held_as)


def setup_inputs(seed: int = 0) -> dict:
    arg_keys = jax.random.split(jax.random.key(seed), 6)
    image_pool = jnp.clip(-1.0 + 3.0 * jax.random.uniform(arg_keys[0], (POOL, CHAN * PIX), jnp.float32) ** block_scale(arg_keys[0], (POOL, CHAN * PIX), ((0, 32),), -0.2, 0.2), -1.0, 2.0).astype(jnp.bfloat16)
    target_index = draw_target_index(jax.random.fold_in(arg_keys[5], 71), 0)
    labels = plant(jax.random.randint(arg_keys[2], (TARGETS,), 0, CLASSES), jax.random.fold_in(arg_keys[2], 1), 0, CLASSES - 1).astype(jnp.int32)
    support = jnp.clip(-1.0 + 3.0 * jax.random.uniform(arg_keys[3], (SUPPORTS, CHAN, PIX), jnp.float32) ** block_scale(arg_keys[3], (SUPPORTS, CHAN, PIX), ((0, 16),), -0.2, 0.2), -1.0, 2.0)
    ridge_coef = bell_draw(arg_keys[4], (SUPPORTS, CLASSES), (SUPPORTS // 4) ** -0.5, 1.5, ((0, 16),), jnp.float32)
    return {"image_pool": image_pool, "target_index": target_index, "labels": labels, "support": support, "ridge_coef": ridge_coef}


WEIGHT_VAR = 2.0
BIAS_VAR = 0.1

def box_sum(values_map):
    column = jnp.arange(SIDE * SIDE) % SIDE
    zero_col = jnp.zeros(values_map.shape[:-1] + (1,), values_map.dtype)
    from_left = jnp.concatenate([zero_col, values_map[..., :-1]], -1)
    from_right = jnp.concatenate([values_map[..., 1:], zero_col], -1)
    row_sum = values_map + jnp.where(column > 0, from_left, 0.0) + jnp.where(column < SIDE - 1, from_right, 0.0)
    zero_row = jnp.zeros(values_map.shape[:-1] + (SIDE,), values_map.dtype)
    from_above = jnp.concatenate([zero_row, row_sum[..., :-SIDE]], -1)
    from_below = jnp.concatenate([row_sum[..., SIDE:], zero_row], -1)
    return (row_sum + from_above + from_below) / 9.0

def self_maps(pixels):
    current = lax.optimization_barrier(jnp.sum(pixels * pixels, axis=1)) / 3.0
    variances = []
    for depth in range(LAYERS):
        variance = WEIGHT_VAR * box_sum(current) + BIAS_VAR
        variances.append(variance)
        current = 2.0 / math.pi * jnp.arcsin(2.0 * variance / (1.0 + 2.0 * variance))
    return variances

def cross_layer(current, target_var, support_var):
    covariance = WEIGHT_VAR * box_sum(current) + BIAS_VAR
    denominator = jnp.sqrt((1.0 + 2.0 * target_var)[:, None, :] * (1.0 + 2.0 * support_var)[None, :, :])
    return 2.0 / math.pi * jnp.arcsin(2.0 * covariance / denominator)

def kernel_rows(targets, support):
    target_vars = self_maps(targets)
    support_vars = self_maps(support)
    current = jnp.einsum('icp,jcp->ijp', targets, support, precision=lax.Precision.HIGHEST) / 3.0
    for depth in range(LAYERS):
        current = cross_layer(current, target_vars[depth], support_vars[depth])
    return lax.optimization_barrier(jnp.mean(current, axis=-1))

def reference(image_pool, target_index, labels, support, ridge_coef):
    images = image_pool[target_index].astype(jnp.float32)
    blocks = images.reshape(N_TGT, TGT_DEV, CHAN, SIDE * SIDE)
    label_blocks = labels.reshape(N_TGT, TGT_DEV)
    classes = jnp.arange(CLASSES)
    loss_scale = float(SIDE * SIDE) / TGT_DEV

    def one_block(running, inputs):
        target_block, block_labels = inputs
        kernel_block, pullback = jax.vjp(lambda points: kernel_rows(target_block, points), support)
        predicted = jnp.dot(kernel_block, ridge_coef, precision=lax.Precision.HIGHEST, preferred_element_type=jnp.float32)
        residual = predicted - (block_labels[:, None] == classes[None, :]).astype(jnp.float32)
        kernel_grad = loss_scale * jnp.dot(residual, ridge_coef.T, precision=lax.Precision.HIGHEST, preferred_element_type=jnp.float32)
        return (running + pullback(kernel_grad)[0], residual)
    support_grad, residual = lax.scan(one_block, jnp.zeros_like(support), (blocks, label_blocks))
    return (residual.reshape(TARGETS, CLASSES), support_grad)
```

```python
import functools
import math

import jax
import jax.numpy as jnp
from jax import lax
from jax.experimental import pallas as pl
from jax.experimental.pallas import tpu as pltpu
from jax.sharding import PartitionSpec as P

LAYERS = 4
HI = lax.Precision.HIGHEST
MESH = pl.DeviceIdType.MESH
F32 = jnp.float32
BF16 = jnp.bfloat16
TWO_PI = 2.0 / math.pi
LANES = 128
SUBL = 8


def arcsin(x):
    a = jnp.abs(x)
    big = a > 0.5
    z = jnp.where(big, 0.5 - 0.5 * a, x * x)
    root = jnp.where(big, z * lax.rsqrt(jnp.maximum(z, 1e-30)), a)
    p = 4.2163199048e-2 * z + 2.4181311049e-2
    p = p * z + 4.5470025998e-2
    p = p * z + 7.4953002686e-2
    p = p * z + 1.6666752422e-1
    p = p * (z * root) + root
    r = jnp.where(big, 0.5 * math.pi - 2.0 * p, p)
    return jnp.where(x < 0.0, -r, r)


def box_rows(x, side):
    pix = x.shape[-1]
    p = lax.broadcasted_iota(jnp.int32, x.shape, 1)
    col = p % side
    row = (
        x
        + jnp.where(col > 0, pltpu.roll(x, 1, 1), 0.0)
        + jnp.where(col < side - 1, pltpu.roll(x, pix - 1, 1), 0.0)
    )
    return (
        row
        + jnp.where(p >= side, pltpu.roll(row, side, 1), 0.0)
        + jnp.where(p < pix - side, pltpu.roll(row, pix - side, 1), 0.0)
    )


def self_vars(self0, side):
    act, out = self0, []
    for depth in range(LAYERS):
        var = (2.0 / 9.0) * box_rows(act, side) + 0.1
        out.append(var)
        if depth < LAYERS - 1:
            act = TWO_PI * arcsin(2.0 * var / (1.0 + 2.0 * var))
    return out


def dot0(a, b, precision=None):
    return lax.dot_general(
        a, b, (((0,), (0,)), ((), ())), precision=precision, preferred_element_type=F32
    )


def split3(x):
    hi = x.astype(BF16)
    rest = x - hi.astype(F32)
    mid = rest.astype(BF16)
    low = (rest - mid.astype(F32)).astype(BF16)
    return hi, mid, low


def kernel(
    dims, idx_ref, lab_ref, pool_ref, sup_ref, ridge_ref, res_ref, grad_ref,
    psend, pown, prec, rsbuf, tbuf, tfull, rall, kbuf, gsend, grecv,
    s8, sexp, rbexp, svar, texp, wbuf, a1, a2, hs, pad_a, pad_b, usum, ut, coef,
    p_s, p_r, rs_s, rs_r, ag_s, ag_r, r_s, r_r, k_s, k_r, g_s, g_r,
):
    n_tgt, n_sup, n_shards, n_chunk, width, side = dims
    ns, chan, pix = sup_ref.shape
    nt = idx_ref.shape[1]
    pool_rows = pool_ref.shape[0]
    classes = ridge_ref.shape[1]
    per_owner = res_ref.shape[1]
    qn = side // SUBL
    mtile = pix // SUBL
    stride_q = (side + 2) * SUBL
    me = lax.axis_index("sup")
    grp = lax.axis_index("tgt")
    half = nt // 2

    barrier = pltpu.get_barrier_semaphore()
    for d in range(1, n_sup):
        pl.semaphore_signal(barrier, inc=1, device_id=(grp, lax.rem(me + d, n_sup)), device_id_type=MESH)
    for d in range(1, n_tgt):
        pl.semaphore_signal(barrier, inc=1, device_id=(lax.rem(grp + d, n_tgt), me), device_id_type=MESH)

    base = (grp * n_sup + me) * pool_rows
    for d in list(range(1, n_tgt)) + [0]:
        g = lax.rem(grp + d, n_tgt)
        ids = idx_ref[pl.ds(g, 1), :] - base
        row_id = lax.broadcasted_iota(jnp.int32, (pool_rows, nt), 0)
        selector = (row_id == ids).astype(F32).astype(BF16)
        for ch in range(n_chunk):
            block = dot0(selector, pool_ref[:, ch * width:(ch + 1) * width]).astype(BF16)
            for h in range(2):
                piece = block[h * half:(h + 1) * half]
                if d == 0:
                    pown[h * n_chunk + ch] = piece
                else:
                    psend[d - 1, h * n_chunk + ch] = piece
        if d == 1:
            pl.semaphore_wait(barrier, n_sup + n_tgt - 2)
        if d > 0:
            pltpu.make_async_remote_copy(
                src_ref=psend.at[d - 1], dst_ref=prec.at[d - 1],
                send_sem=p_s.at[d - 1], recv_sem=p_r.at[d - 1],
                device_id=(g, me), device_id_type=MESH,
            ).start()

    def tgt_copy(d):
        return pltpu.make_async_remote_copy(
            src_ref=psend.at[d - 1], dst_ref=prec.at[d - 1],
            send_sem=p_s.at[d - 1], recv_sem=p_r.at[d - 1],
            device_id=(lax.rem(grp + d, n_tgt), me), device_id_type=MESH,
        )

    for d in range(1, n_tgt):
        tgt_copy(d).wait_recv()
    total = pown[...]
    for d in range(1, n_tgt):
        total = total + prec[d - 1]
    pown[...] = total

    def rs_copy(d):
        peer = lax.rem(me + d, n_sup)
        return peer, pltpu.make_async_remote_copy(
            src_ref=pown.at[lax.rem(peer, n_shards)], dst_ref=rsbuf.at[d - 1],
            send_sem=rs_s.at[d - 1], recv_sem=rs_r.at[d - 1],
            device_id=(grp, peer), device_id_type=MESH,
        )

    def when(cond, fn):
        if n_shards == n_sup:
            fn()
        else:
            pl.when(cond)(fn)

    for d in range(1, n_sup):
        peer, copy = rs_copy(d)
        when(peer < n_shards, copy.start)

    for c in range(chan):
        s8[c, ns:, :] = jnp.zeros((SUBL - ns, pix), F32)
        for j in range(ns):
            s8[c, j:j + 1, :] = sup_ref[j, c:c + 1, :]
    sup_self = s8[0] * s8[0]
    for c in range(1, chan):
        sup_self = sup_self + s8[c] * s8[c]
    svs = self_vars(sup_self / chan, side)
    row8 = lax.broadcasted_iota(jnp.int32, (SUBL, LANES), 0)
    lane8 = lax.broadcasted_iota(jnp.int32, (SUBL, LANES), 1)
    hot_j = (row8 == lane8 // nt).astype(F32)
    for depth in range(LAYERS):
        svar[depth] = svs[depth]
    for s in range(SUBL):
        cut = slice(s * mtile, (s + 1) * mtile)
        for c in range(chan):
            sexp[c, cut, :] = dot0(s8[c, :, cut], hot_j, HI)
        for depth in range(LAYERS):
            rbexp[depth, cut, :] = dot0(lax.rsqrt(1.0 + 2.0 * svs[depth][:, cut]), hot_j, HI)
    zero_tile = jnp.zeros((SUBL, LANES), F32)
    for buf in (pad_a, pad_b):
        for q in range(qn):
            buf[q * stride_q:q * stride_q + SUBL, :] = zero_tile
            buf[(q + 1) * stride_q - SUBL:(q + 1) * stride_q, :] = zero_tile

    def ag_copy(d):
        return pltpu.make_async_remote_copy(
            src_ref=tbuf.at[lax.rem(me, n_shards)], dst_ref=tbuf.at[lax.rem(me, n_shards)],
            send_sem=ag_s.at[d - 1], recv_sem=ag_r.at[d - 1],
            device_id=(grp, lax.rem(me + d, n_sup)), device_id_type=MESH,
        )

    def own_shard():
        acc = pown[me].astype(F32)
        for d in range(1, n_sup):
            rs_copy(d)[1].wait_recv()
            acc = acc + rsbuf[d - 1].astype(F32)
        tbuf[me] = acc.astype(BF16)
        for d in range(1, n_sup):
            ag_copy(d).start()

    when(me < n_shards, own_shard)

    def ridge_copy(d):
        return pltpu.make_async_remote_copy(
            src_ref=ridge_ref, dst_ref=rall.at[me],
            send_sem=r_s.at[d - 1], recv_sem=r_r.at[d - 1],
            device_id=(grp, lax.rem(me + d, n_sup)), device_id_type=MESH,
        )

    for d in range(1, n_sup):
        ridge_copy(d).start()
    rall[me] = ridge_ref[...]
    for d in range(1, n_sup):
        when(lax.rem(me - d + n_sup, n_sup) < n_shards, ag_copy(d).wait_recv)

    for h in range(2):
        for ch in range(n_chunk):
            tfull[h * half:(h + 1) * half, ch * width:(ch + 1) * width] = tbuf[h * n_chunk + ch]

    tgt_self = jnp.zeros((nt, pix), F32)
    for c in range(chan):
        t = tfull[:, c * pix:(c + 1) * pix].astype(F32)
        tgt_self = tgt_self + t * t
    tvs = self_vars(tgt_self / chan, side)
    row_t = lax.broadcasted_iota(jnp.int32, (nt, LANES), 0)
    lane_t = lax.broadcasted_iota(jnp.int32, (nt, LANES), 1)
    hot_i = (row_t == lane_t % nt).astype(F32).astype(BF16)
    hot_i3 = jnp.concatenate([hot_i] * 3, axis=0)
    for s in range(SUBL):
        cut = slice(s * mtile, (s + 1) * mtile)
        pair0 = jnp.zeros((mtile, LANES), F32)
        for c in range(chan):
            t = dot0(tfull[:, c * pix + s * mtile:c * pix + (s + 1) * mtile], hot_i)
            texp[c, pl.ds(s, mtile, stride=SUBL), :] = t
            pair0 = pair0 + t * sexp[c, cut, :]
        pair0 = pair0 / chan
        for q in range(qn):
            pad_a[pl.ds(q * stride_q + SUBL + s, side, stride=SUBL), :] = pair0[q * side:(q + 1) * side]
        for depth in range(LAYERS):
            inv = lax.rsqrt(1.0 + 2.0 * tvs[depth][:, cut])
            wide = dot0(jnp.concatenate(split3(inv), axis=0), hot_i3)
            wbuf[depth, pl.ds(s, mtile, stride=SUBL), :] = wide * rbexp[depth, cut, :]

    sub = lax.broadcasted_iota(jnp.int32, (SUBL, LANES), 0)

    def box_column(buf, c):
        sums = []
        for q in range(qn):
            def at(k):
                return buf[pl.ds(pl.multiple_of(q * stride_q + (c + k) * SUBL, SUBL), SUBL), :]
            sums.append(at(0) + at(1) + at(2))
        up = jnp.where(sub > 0, pltpu.roll(sums[-1], 1, 0), 0.0)
        down = jnp.where(sub < SUBL - 1, pltpu.roll(sums[0], SUBL - 1, 0), 0.0)
        ext = [up] + sums + [down]
        return [ext[q] + ext[q + 1] + ext[q + 2] for q in range(qn)]

    def tile(q, c):
        return pl.ds(pl.multiple_of((q * side + c) * SUBL, SUBL), SUBL)

    def padded(q, c):
        return pl.ds(pl.multiple_of(q * stride_q + (c + 1) * SUBL, SUBL), SUBL)

    def forward(depth, src, dst):
        def body(c, acc):
            sums = box_column(src, c)
            for q in range(qn):
                w = wbuf[depth, tile(q, c), :]
                ang = (sums[q] * (4.0 / 9.0) + 0.2) * w
                der = TWO_PI * lax.rsqrt(1.0 - ang * ang)
                a1[depth, tile(q, c), :] = der * w
                a2[depth, tile(q, c), :] = der * ang
                pair = TWO_PI * arcsin(ang)
                if dst is None:
                    acc = acc + pair
                else:
                    dst[padded(q, c), :] = pair
            return acc
        return lax.fori_loop(0, side, body, zero_tile, unroll=4)

    bufs = (pad_a, pad_b)
    for depth in range(LAYERS - 1):
        forward(depth, bufs[depth % 2], bufs[(depth + 1) % 2])
    acc = forward(LAYERS - 1, bufs[(LAYERS - 1) % 2], None)
    krow = jnp.sum(acc, axis=0, keepdims=True) / pix
    kbuf[me] = jnp.broadcast_to(krow, (SUBL, LANES))

    def k_copy(d):
        return pltpu.make_async_remote_copy(
            src_ref=kbuf.at[me], dst_ref=kbuf.at[me],
            send_sem=k_s.at[d - 1], recv_sem=k_r.at[d - 1],
            device_id=(grp, lax.rem(me + d, n_sup)), device_id_type=MESH,
        )

    for d in range(1, n_sup):
        k_copy(d).start()

    for d in range(1, n_sup):
        ridge_copy(d).wait_recv()
    ridge_rows = jnp.concatenate([rall[:, j, :] for j in range(ns)], axis=0)
    mine = jnp.concatenate([ridge_ref[...], jnp.zeros((SUBL - ns, classes), F32)], axis=0)
    gram = lax.dot_general(
        ridge_rows, mine, (((1,), (1,)), ((), ())), precision=HI, preferred_element_type=F32
    )
    wide_gram = jnp.dot(gram, hot_j, precision=HI, preferred_element_type=F32)
    lane_k = lax.broadcasted_iota(jnp.int32, (n_sup, LANES), 1) // nt
    for d in range(ns):
        acc_c = jnp.zeros((n_sup, LANES), F32)
        for j in range(ns):
            acc_c = jnp.where((lane_k + d) % ns == j, wide_gram[j * n_sup:(j + 1) * n_sup], acc_c)
        coef[d] = acc_c
    labels = lab_ref[...].astype(F32)
    lab_row = jnp.dot(
        jnp.broadcast_to(labels, (SUBL, nt)), hot_i.astype(F32), precision=HI, preferred_element_type=F32
    )[0:1]
    class_id = lax.broadcasted_iota(jnp.int32, (classes, LANES), 0).astype(F32)
    label_hot = (class_id == lab_row).astype(F32)
    picked = jnp.dot(mine, label_hot, precision=HI, preferred_element_type=F32)
    lab_term = jnp.sum(picked * hot_j, axis=0, keepdims=True)

    for d in range(1, n_sup):
        k_copy(d).wait_recv()
    kall = kbuf[:, 0, :]
    kg = kall * coef[0]
    for d in range(1, ns):
        kg = kg + pltpu.roll(kall, LANES - d * nt, 1) * coef[d]
    kg = jnp.sum(kg, axis=0, keepdims=True) - lab_term
    scale = float(side * side) / nt / pix
    top = jnp.broadcast_to(kg * scale, (SUBL, LANES))

    def backward(depth, src, dst):
        def body(c, carry):
            if src is None:
                grads = [top] * qn
            else:
                grads = [x * (4.0 / 9.0) for x in box_column(src, c)]
            for q in range(qn):
                dst[padded(q, c), :] = grads[q] * a1[depth, tile(q, c), :]
                hs[depth, tile(q, c), :] = grads[q] * a2[depth, tile(q, c), :]
            return carry
        lax.fori_loop(0, side, body, 0, unroll=4)

    src = None
    for step, depth in enumerate(reversed(range(LAYERS))):
        backward(depth, src, bufs[step % 2])
        src = bufs[step % 2]

    def input_grad(c, carry):
        grads = [x * (4.0 / 9.0 / chan) for x in box_column(src, c)]
        for q in range(qn):
            for ch in range(chan):
                hs[LAYERS + ch, tile(q, c), :] = grads[q] * texp[ch, tile(q, c), :]
        return carry
    lax.fori_loop(0, side, input_grad, 0, unroll=4)

    row_l = lax.broadcasted_iota(jnp.int32, (LANES, LANES), 0)
    col_l = lax.broadcasted_iota(jnp.int32, (LANES, LANES), 1)
    gather = [
        (col_l == a * SUBL + row_l // nt).astype(F32).astype(BF16) for a in range(LAYERS + chan)
    ]
    gather = [jnp.concatenate([x, x], axis=0) for x in gather]
    blk = 256
    for b in range(pix // blk):
        total = jnp.zeros((blk, LANES), F32)
        for a in range(LAYERS + chan):
            x = hs[a, b * blk:(b + 1) * blk, :]
            hi = x.astype(BF16)
            low = (x - hi.astype(F32)).astype(BF16)
            total = total + jnp.dot(
                jnp.concatenate([hi, low], axis=1), gather[a], preferred_element_type=F32
            )
        usum[b * blk:(b + 1) * blk, :] = total
    for s in range(SUBL):
        turned = usum[pl.ds(s, mtile, stride=SUBL), :].T
        ut[:, s * mtile:(s + 1) * mtile] = turned[:(LAYERS + chan) * SUBL]

    dact = None
    for depth in reversed(range(LAYERS)):
        var = svar[depth]
        dvar = -ut[depth * SUBL:(depth + 1) * SUBL, :] / (1.0 + 2.0 * var)
        if dact is not None:
            dvar = dvar + dact * (2.0 * TWO_PI) * lax.rsqrt(1.0 + 4.0 * var) / (1.0 + 2.0 * var)
        dact = (2.0 / 9.0) * box_rows(dvar, side)
    for c in range(chan):
        a = LAYERS + c
        gsend[c] = ut[a * SUBL:(a + 1) * SUBL, :] + dact * (2.0 / chan) * s8[c]

    def g_copy(d):
        return pltpu.make_async_remote_copy(
            src_ref=gsend, dst_ref=grecv.at[d - 1],
            send_sem=g_s.at[d - 1], recv_sem=g_r.at[d - 1],
            device_id=(lax.rem(grp + d, n_tgt), me), device_id_type=MESH,
        )

    for d in range(1, n_tgt):
        g_copy(d).start()

    first = me * per_owner
    chunk = pl.multiple_of((first // LANES) * LANES, LANES)
    pred = jnp.zeros((nt, LANES), F32)
    for j in range(ns):
        pred = pred + dot0(kall[:, j * nt:(j + 1) * nt], rall[:, j, pl.ds(chunk, LANES)], HI)
    lab_col = jnp.sum(jnp.where(row_t == lane_t, lab_row, 0.0), axis=1, keepdims=True)
    pred = pred - ((lane_t + chunk).astype(F32) == lab_col).astype(F32)
    pred = pltpu.roll(pred, lax.rem(LANES - first % LANES, LANES), 1)
    res_ref[...] = pred[:, :per_owner]

    for d in range(1, n_tgt):
        g_copy(d).wait_recv()
    for c in range(chan):
        terms = gsend[c]
        if n_tgt == 2:
            terms = terms + grecv[0, c]
        else:
            terms = jnp.zeros_like(terms)
            for g in range(n_tgt):
                dist = lax.rem(grp - g + n_tgt, n_tgt)
                part = grecv[jnp.maximum(dist - 1, 0), c]
                terms = terms + jnp.where(dist == 0, gsend[c], part)
        for j in range(ns):
            grad_ref[j, c:c + 1, :] = terms[j:j + 1]

    for d in range(1, n_tgt):
        tgt_copy(d).wait_send()
        g_copy(d).wait_send()
    for d in range(1, n_sup):
        peer, copy = rs_copy(d)
        when(peer < n_shards, copy.wait_send)
        when(me < n_shards, ag_copy(d).wait_send)
        ridge_copy(d).wait_send()
        k_copy(d).wait_send()


def solution(mesh):
    n_tgt, n_sup = mesh.shape["tgt"], mesh.shape["sup"]

    def local(image_pool, target_index, labels, support, ridge_coef):
        nt = labels.shape[0]
        ns, chan, pix = support.shape
        side = math.isqrt(pix)
        classes = ridge_coef.shape[1]
        per_owner = classes // n_sup
        lane_tiles = chan * pix // LANES
        n_chunk = max(k for k in range(1, lane_tiles + 1) if lane_tiles % k == 0 and 2 * k <= n_sup)
        n_shards = 2 * n_chunk
        width = chan * pix // n_chunk
        dims = (n_tgt, n_sup, n_shards, n_chunk, width, side)
        half = nt // 2
        pad_rows = (side // SUBL) * (side + 2) * SUBL
        shard = (n_shards, half, width)
        dma = pltpu.SemaphoreType.DMA
        sems = []
        for n in (n_tgt, n_sup, n_sup, n_sup, n_sup, n_tgt):
            sems += [dma((n - 1,)), dma((n - 1,))]
        f32map = lambda n: pltpu.VMEM((n, pix, LANES), F32)
        scratch = [
            pltpu.VMEM((n_tgt - 1,) + shard, BF16),
            pltpu.VMEM(shard, BF16),
            pltpu.VMEM((n_tgt - 1,) + shard, BF16),
            pltpu.VMEM((n_sup - 1, half, width), BF16),
            pltpu.VMEM(shard, BF16),
            pltpu.VMEM((nt, chan * pix), BF16),
            pltpu.VMEM((n_sup, ns, classes), F32),
            pltpu.VMEM((n_sup, SUBL, LANES), F32),
            pltpu.VMEM((chan, SUBL, pix), F32),
            pltpu.VMEM((n_tgt - 1, chan, SUBL, pix), F32),
            pltpu.VMEM((chan, SUBL, pix), F32),
            f32map(chan),
            f32map(LAYERS),
            pltpu.VMEM((LAYERS, SUBL, pix), F32),
            f32map(chan),
            f32map(LAYERS),
            f32map(LAYERS),
            f32map(LAYERS),
            f32map(LAYERS + chan),
            pltpu.VMEM((pad_rows, LANES), F32),
            pltpu.VMEM((pad_rows, LANES), F32),
            pltpu.VMEM((pix, LANES), F32),
            pltpu.VMEM(((LAYERS + chan) * SUBL, pix), F32),
            pltpu.VMEM((ns, n_sup, LANES), F32),
        ] + sems
        vmem = pl.BlockSpec(memory_space=pltpu.VMEM)
        return pl.pallas_call(
            functools.partial(kernel, dims),
            out_shape=(
                jax.ShapeDtypeStruct((nt, per_owner), F32),
                jax.ShapeDtypeStruct(support.shape, F32),
            ),
            in_specs=[vmem] * 5,
            out_specs=(vmem, vmem),
            scratch_shapes=scratch,
            compiler_params=pltpu.CompilerParams(collective_id=0, has_side_effects=True, vmem_limit_bytes=60000 * 1024),
        )(target_index.reshape(n_tgt, nt), labels.reshape(1, nt), image_pool, support, ridge_coef)

    in_specs = (P(("tgt", "sup"), None), P(), P("tgt"), P("sup", None, None), P("sup", None))
    out_specs = (P("tgt", "sup"), P("sup", None, None))
    return jax.shard_map(local, mesh=mesh, in_specs=in_specs, out_specs=out_specs, check_vma=False)
```

```python
import functools
import math

import jax
import jax.numpy as jnp
from jax import lax
from jax.experimental import pallas as pl
from jax.experimental.pallas import tpu as pltpu
from jax.sharding import PartitionSpec as P

LAYERS = 4
HI = lax.Precision.HIGHEST
MESH = pl.DeviceIdType.MESH
F32 = jnp.float32
BF16 = jnp.bfloat16
TWO_PI = 2.0 / math.pi
LANES = 128
SUBL = 8


def arcsin(x):
    a = jnp.abs(x)
    big = a > 0.5
    z = jnp.where(big, 0.5 - 0.5 * a, x * x)
    root = jnp.where(big, z * lax.rsqrt(jnp.maximum(z, 1e-30)), a)
    p = 4.2163199048e-2 * z + 2.4181311049e-2
    p = p * z + 4.5470025998e-2
    p = p * z + 7.4953002686e-2
    p = p * z + 1.6666752422e-1
    p = p * (z * root) + root
    r = jnp.where(big, 0.5 * math.pi - 2.0 * p, p)
    return jnp.where(x < 0.0, -r, r)


def box_rows(x, side):
    pix = x.shape[-1]
    p = lax.broadcasted_iota(jnp.int32, x.shape, 1)
    col = p % side
    row = (
        x
        + jnp.where(col > 0, pltpu.roll(x, 1, 1), 0.0)
        + jnp.where(col < side - 1, pltpu.roll(x, pix - 1, 1), 0.0)
    )
    return (
        row
        + jnp.where(p >= side, pltpu.roll(row, side, 1), 0.0)
        + jnp.where(p < pix - side, pltpu.roll(row, pix - side, 1), 0.0)
    )


def self_vars(self0, side):
    act, out = self0, []
    for depth in range(LAYERS):
        var = (2.0 / 9.0) * box_rows(act, side) + 0.1
        out.append(var)
        if depth < LAYERS - 1:
            act = TWO_PI * arcsin(2.0 * var / (1.0 + 2.0 * var))
    return out


def dot0(a, b, precision=None):
    return lax.dot_general(
        a, b, (((0,), (0,)), ((), ())), precision=precision, preferred_element_type=F32
    )


def split3(x):
    hi = x.astype(BF16)
    rest = x - hi.astype(F32)
    mid = rest.astype(BF16)
    low = (rest - mid.astype(F32)).astype(BF16)
    return hi, mid, low


def kernel(
    dims, idx_ref, lab_ref, pool_ref, sup_ref, ridge_ref, res_ref, grad_ref,
    psend, pown, prec, rsbuf, tbuf, tfull, rcls, rown, psrc, pdst, kbuf, gsend, grecv,
    s8, sexp, rbexp, svar, texp, wbuf, a1, a2, hs, pad_a, pad_b, usum, ut, coef,
    p_s, p_r, rs_s, rs_r, ag_s, ag_r, r_s, r_r, q_s, q_r, k_s, k_r, g_s, g_r,
):
    n_tgt, n_sup, n_shards, n_chunk, width, side = dims
    chan, ns, pix = sup_ref.shape
    nt = res_ref.shape[0]
    pool_rows = pool_ref.shape[0]
    classes = ridge_ref.shape[1]
    per_owner = res_ref.shape[1]
    qn = side // SUBL
    mtile = pix // SUBL
    stride_q = (side + 2) * SUBL
    me = lax.axis_index("sup")
    grp = lax.axis_index("tgt")
    half = nt // 2

    barrier = pltpu.get_barrier_semaphore()
    for d in range(1, n_sup):
        pl.semaphore_signal(barrier, inc=1, device_id=(grp, lax.rem(me + d, n_sup)), device_id_type=MESH)
    for d in range(1, n_tgt):
        pl.semaphore_signal(barrier, inc=1, device_id=(lax.rem(grp + d, n_tgt), me), device_id_type=MESH)

    base = (grp * n_sup + me) * pool_rows
    ids = idx_ref[...] - base
    row_id = lax.broadcasted_iota(jnp.int32, (pool_rows, n_tgt * nt), 0)
    selector = (row_id == ids).astype(F32).astype(BF16)
    for ch in range(n_chunk):
        block = dot0(selector, pool_ref[:, ch * width:(ch + 1) * width]).astype(BF16)
        for g in range(n_tgt):
            for h in range(2):
                psend[g, h * n_chunk + ch] = block[g * nt + h * half:g * nt + (h + 1) * half]
    pl.semaphore_wait(barrier, n_sup + n_tgt - 2)

    def class_tile(k):
        return pl.ds(pl.multiple_of(((k * per_owner) // LANES) * LANES, LANES), LANES)

    def ridge_copy(d):
        peer = lax.rem(me + d, n_sup)
        return pltpu.make_async_remote_copy(
            src_ref=ridge_ref.at[:, class_tile(peer)], dst_ref=rcls.at[me],
            send_sem=r_s.at[d - 1], recv_sem=r_r.at[d - 1],
            device_id=(grp, peer), device_id_type=MESH,
        )

    def tgt_copy(d):
        return pltpu.make_async_remote_copy(
            src_ref=psend.at[lax.rem(grp + d, n_tgt)], dst_ref=prec.at[d - 1],
            send_sem=p_s.at[d - 1], recv_sem=p_r.at[d - 1],
            device_id=(lax.rem(grp + d, n_tgt), me), device_id_type=MESH,
        )

    for d in range(1, n_tgt):
        tgt_copy(d).start()
    for d in range(1, n_sup):
        ridge_copy(d).start()
    rcls[me] = ridge_ref[:, class_tile(me)]
    for d in range(1, n_tgt):
        tgt_copy(d).wait_recv()
    total = psend[grp]
    for d in range(1, n_tgt):
        total = total + prec[d - 1]
    pown[...] = total

    def rs_copy(d):
        peer = lax.rem(me + d, n_sup)
        return peer, pltpu.make_async_remote_copy(
            src_ref=pown.at[lax.rem(peer, n_shards)], dst_ref=rsbuf.at[d - 1],
            send_sem=rs_s.at[d - 1], recv_sem=rs_r.at[d - 1],
            device_id=(grp, peer), device_id_type=MESH,
        )

    def when(cond, fn):
        if n_shards == n_sup:
            fn()
        else:
            pl.when(cond)(fn)

    for d in range(1, n_sup):
        peer, copy = rs_copy(d)
        when(peer < n_shards, copy.start)

    for c in range(chan):
        s8[c, ns:, :] = jnp.zeros((SUBL - ns, pix), F32)
        s8[c, :ns, :] = sup_ref[c]
    sup_self = s8[0] * s8[0]
    for c in range(1, chan):
        sup_self = sup_self + s8[c] * s8[c]
    svs = self_vars(sup_self / chan, side)
    row8 = lax.broadcasted_iota(jnp.int32, (SUBL, LANES), 0)
    lane8 = lax.broadcasted_iota(jnp.int32, (SUBL, LANES), 1)
    hot_j = (row8 == lane8 // nt).astype(F32)
    for depth in range(LAYERS):
        svar[depth] = svs[depth]
    zero_tile = jnp.zeros((SUBL, LANES), F32)
    for buf in (pad_a, pad_b):
        for q in range(qn):
            buf[q * stride_q:q * stride_q + SUBL, :] = zero_tile
            buf[(q + 1) * stride_q - SUBL:(q + 1) * stride_q, :] = zero_tile

    def ag_copy(d):
        return pltpu.make_async_remote_copy(
            src_ref=tbuf.at[lax.rem(me, n_shards)], dst_ref=tbuf.at[lax.rem(me, n_shards)],
            send_sem=ag_s.at[d - 1], recv_sem=ag_r.at[d - 1],
            device_id=(grp, lax.rem(me + d, n_sup)), device_id_type=MESH,
        )

    def own_shard():
        acc = pown[me].astype(F32)
        for d in range(1, n_sup):
            rs_copy(d)[1].wait_recv()
            acc = acc + rsbuf[d - 1].astype(F32)
        tbuf[me] = acc.astype(BF16)
        for d in range(1, n_sup):
            ag_copy(d).start()

    when(me < n_shards, own_shard)

    for s in range(SUBL):
        cut = slice(s * mtile, (s + 1) * mtile)
        for c in range(chan):
            sexp[c, cut, :] = dot0(s8[c, :, cut], hot_j, HI)
        for depth in range(LAYERS):
            rbexp[depth, cut, :] = dot0(lax.rsqrt(1.0 + 2.0 * svs[depth][:, cut]), hot_j, HI)

    first = me * per_owner
    chunk = (first // LANES) * LANES
    lane_c = lax.broadcasted_iota(jnp.int32, (ns, LANES), 1) + chunk
    own_class = (lane_c >= first) & (lane_c < first + per_owner)
    for d in range(1, n_sup):
        ridge_copy(d).wait_recv()
    for k in range(n_sup):
        rown[k, :ns, :] = jnp.where(own_class, rcls[k], 0.0)
        rown[k, ns:, :] = jnp.zeros((SUBL - ns, LANES), F32)
    rows = rown[...].reshape(n_sup * SUBL, LANES)
    psrc[...] = lax.dot_general(
        rows, rows, (((1,), (1,)), ((), ())), precision=HI, preferred_element_type=F32
    ).reshape(n_sup, SUBL, n_sup * SUBL)

    def gram_copy(d):
        peer = lax.rem(me + d, n_sup)
        return pltpu.make_async_remote_copy(
            src_ref=psrc.at[peer], dst_ref=pdst.at[d - 1],
            send_sem=q_s.at[d - 1], recv_sem=q_r.at[d - 1],
            device_id=(grp, peer), device_id_type=MESH,
        )

    for d in range(1, n_sup):
        gram_copy(d).start()
    row_t = lax.broadcasted_iota(jnp.int32, (nt, LANES), 0)
    lane_t = lax.broadcasted_iota(jnp.int32, (nt, LANES), 1)
    hot_i = (row_t == lane_t % nt).astype(F32).astype(BF16)
    mine = jnp.concatenate([ridge_ref[...], jnp.zeros((SUBL - ns, classes), F32)], axis=0)
    labels = lab_ref[...].astype(F32)
    lab_row = jnp.dot(
        jnp.broadcast_to(labels, (SUBL, nt)), hot_i.astype(F32), precision=HI, preferred_element_type=F32
    )[0:1]
    class_id = lax.broadcasted_iota(jnp.int32, (classes, LANES), 0).astype(F32)
    label_hot = (class_id == lab_row).astype(F32)
    picked = jnp.dot(mine, label_hot, precision=HI, preferred_element_type=F32)
    lab_term = jnp.sum(picked * hot_j, axis=0, keepdims=True)

    for d in range(1, n_sup):
        when(lax.rem(me - d + n_sup, n_sup) < n_shards, ag_copy(d).wait_recv)

    for h in range(2):
        for ch in range(n_chunk):
            tfull[h * half:(h + 1) * half, ch * width:(ch + 1) * width] = tbuf[h * n_chunk + ch]

    tgt_self = jnp.zeros((nt, pix), F32)
    for c in range(chan):
        t = tfull[:, c * pix:(c + 1) * pix].astype(F32)
        tgt_self = tgt_self + t * t
    tvs = self_vars(tgt_self / chan, side)
    hot_i3 = jnp.concatenate([hot_i] * 3, axis=0)
    for s in range(SUBL):
        cut = slice(s * mtile, (s + 1) * mtile)
        pair0 = jnp.zeros((mtile, LANES), F32)
        for c in range(chan):
            t = dot0(tfull[:, c * pix + s * mtile:c * pix + (s + 1) * mtile], hot_i)
            texp[c, pl.ds(s, mtile, stride=SUBL), :] = t
            pair0 = pair0 + t * sexp[c, cut, :]
        pair0 = pair0 / chan
        for q in range(qn):
            pad_a[pl.ds(q * stride_q + SUBL + s, side, stride=SUBL), :] = pair0[q * side:(q + 1) * side]
        for depth in range(LAYERS):
            inv = lax.rsqrt(1.0 + 2.0 * tvs[depth][:, cut])
            wide = dot0(jnp.concatenate(split3(inv), axis=0), hot_i3)
            wbuf[depth, pl.ds(s, mtile, stride=SUBL), :] = wide * rbexp[depth, cut, :]

    sub = lax.broadcasted_iota(jnp.int32, (SUBL, LANES), 0)

    def box_column(buf, c):
        sums = []
        for q in range(qn):
            def at(k):
                return buf[pl.ds(pl.multiple_of(q * stride_q + (c + k) * SUBL, SUBL), SUBL), :]
            sums.append(at(0) + at(1) + at(2))
        up = jnp.where(sub > 0, pltpu.roll(sums[-1], 1, 0), 0.0)
        down = jnp.where(sub < SUBL - 1, pltpu.roll(sums[0], SUBL - 1, 0), 0.0)
        ext = [up] + sums + [down]
        return [ext[q] + ext[q + 1] + ext[q + 2] for q in range(qn)]

    def tile(q, c):
        return pl.ds(pl.multiple_of((q * side + c) * SUBL, SUBL), SUBL)

    def padded(q, c):
        return pl.ds(pl.multiple_of(q * stride_q + (c + 1) * SUBL, SUBL), SUBL)

    def forward(depth, src, dst):
        def body(c, acc):
            sums = box_column(src, c)
            for q in range(qn):
                w = wbuf[depth, tile(q, c), :]
                ang = (sums[q] * (4.0 / 9.0) + 0.2) * w
                der = TWO_PI * lax.rsqrt(1.0 - ang * ang)
                a1[depth, tile(q, c), :] = der * w
                a2[depth, tile(q, c), :] = der * ang
                pair = TWO_PI * arcsin(ang)
                if dst is None:
                    acc = acc + pair
                else:
                    dst[padded(q, c), :] = pair
            return acc
        return lax.fori_loop(0, side, body, zero_tile, unroll=4)

    bufs = (pad_a, pad_b)
    for depth in range(LAYERS - 1):
        forward(depth, bufs[depth % 2], bufs[(depth + 1) % 2])
    acc = forward(LAYERS - 1, bufs[(LAYERS - 1) % 2], None)
    krow = jnp.sum(acc, axis=0, keepdims=True) / pix
    krows = jnp.broadcast_to(krow, (SUBL, LANES))
    turn = (row8 + SUBL * ns - lane8 // nt) % ns
    ktile = krows
    for d in range(1, ns):
        ktile = jnp.where(turn == d, pltpu.roll(krows, LANES - d * nt, 1), ktile)
    kbuf[me] = ktile

    def k_copy(d):
        return pltpu.make_async_remote_copy(
            src_ref=kbuf.at[me], dst_ref=kbuf.at[me],
            send_sem=k_s.at[d - 1], recv_sem=k_r.at[d - 1],
            device_id=(grp, lax.rem(me + d, n_sup)), device_id_type=MESH,
        )

    for d in range(1, n_sup):
        k_copy(d).start()

    gram = psrc[me]
    for d in range(1, n_sup):
        gram_copy(d).wait_recv()
        gram = gram + pdst[d - 1]
    coef[...] = dot0(gram, hot_j, HI)

    for d in range(1, n_sup):
        k_copy(d).wait_recv()
    kall = kbuf[...].reshape(n_sup * SUBL, LANES)
    kg = jnp.sum(kall * coef[...], axis=0, keepdims=True) - lab_term
    scale = float(side * side) / nt / pix
    top = jnp.broadcast_to(kg * scale, (SUBL, LANES))

    def backward(depth, src, dst):
        def body(c, carry):
            if src is None:
                grads = [top] * qn
            else:
                grads = [x * (4.0 / 9.0) for x in box_column(src, c)]
            for q in range(qn):
                dst[padded(q, c), :] = grads[q] * a1[depth, tile(q, c), :]
                hs[depth, tile(q, c), :] = grads[q] * a2[depth, tile(q, c), :]
            return carry
        lax.fori_loop(0, side, body, 0, unroll=4)

    src = None
    for step, depth in enumerate(reversed(range(LAYERS))):
        backward(depth, src, bufs[step % 2])
        src = bufs[step % 2]

    def input_grad(c, carry):
        grads = [x * (4.0 / 9.0 / chan) for x in box_column(src, c)]
        for q in range(qn):
            for ch in range(chan):
                hs[LAYERS + ch, tile(q, c), :] = grads[q] * texp[ch, tile(q, c), :]
        return carry
    lax.fori_loop(0, side, input_grad, 0, unroll=4)

    row_l = lax.broadcasted_iota(jnp.int32, (LANES, LANES), 0)
    col_l = lax.broadcasted_iota(jnp.int32, (LANES, LANES), 1)
    gather = [
        (col_l == a * SUBL + row_l // nt).astype(F32).astype(BF16) for a in range(LAYERS + chan)
    ]
    gather = [jnp.concatenate([x, x], axis=0) for x in gather]
    blk = 256
    for b in range(pix // blk):
        total = jnp.zeros((blk, LANES), F32)
        for a in range(LAYERS + chan):
            x = hs[a, b * blk:(b + 1) * blk, :]
            hi = x.astype(BF16)
            low = (x - hi.astype(F32)).astype(BF16)
            total = total + jnp.dot(
                jnp.concatenate([hi, low], axis=1), gather[a], preferred_element_type=F32
            )
        usum[b * blk:(b + 1) * blk, :] = total
    for s in range(SUBL):
        turned = usum[pl.ds(s, mtile, stride=SUBL), :].T
        ut[:, s * mtile:(s + 1) * mtile] = turned[:(LAYERS + chan) * SUBL]

    dact = None
    for depth in reversed(range(LAYERS)):
        var = svar[depth]
        dvar = -ut[depth * SUBL:(depth + 1) * SUBL, :] / (1.0 + 2.0 * var)
        if dact is not None:
            dvar = dvar + dact * (2.0 * TWO_PI) * lax.rsqrt(1.0 + 4.0 * var) / (1.0 + 2.0 * var)
        dact = (2.0 / 9.0) * box_rows(dvar, side)
    for c in range(chan):
        a = LAYERS + c
        gsend[c] = ut[a * SUBL:(a + 1) * SUBL, :] + dact * (2.0 / chan) * s8[c]

    def g_copy(d):
        return pltpu.make_async_remote_copy(
            src_ref=gsend, dst_ref=grecv.at[d - 1],
            send_sem=g_s.at[d - 1], recv_sem=g_r.at[d - 1],
            device_id=(lax.rem(grp + d, n_tgt), me), device_id_type=MESH,
        )

    for d in range(1, n_tgt):
        g_copy(d).start()

    pred = dot0(kall[:, :nt], rows, HI)
    lab_col = jnp.sum(jnp.where(row_t == lane_t, lab_row, 0.0), axis=1, keepdims=True)
    pred = pred - ((lane_t + chunk).astype(F32) == lab_col).astype(F32)
    pred = pltpu.roll(pred, lax.rem(LANES - first % LANES, LANES), 1)
    res_ref[...] = pred[:, :per_owner]

    for d in range(1, n_tgt):
        g_copy(d).wait_recv()
    for c in range(chan):
        terms = gsend[c]
        if n_tgt == 2:
            terms = terms + grecv[0, c]
        else:
            terms = jnp.zeros_like(terms)
            for g in range(n_tgt):
                dist = lax.rem(grp - g + n_tgt, n_tgt)
                part = grecv[jnp.maximum(dist - 1, 0), c]
                terms = terms + jnp.where(dist == 0, gsend[c], part)
        grad_ref[c] = terms[:ns]

    for d in range(1, n_tgt):
        tgt_copy(d).wait_send()
        g_copy(d).wait_send()
    for d in range(1, n_sup):
        peer, copy = rs_copy(d)
        when(peer < n_shards, copy.wait_send)
        when(me < n_shards, ag_copy(d).wait_send)
        ridge_copy(d).wait_send()
        gram_copy(d).wait_send()
        k_copy(d).wait_send()


def solution(mesh):
    n_tgt, n_sup = mesh.shape["tgt"], mesh.shape["sup"]

    def local(image_pool, target_index, labels, support, ridge_coef):
        nt = labels.shape[0]
        ns, chan, pix = support.shape
        side = math.isqrt(pix)
        classes = ridge_coef.shape[1]
        per_owner = classes // n_sup
        lane_tiles = chan * pix // LANES
        n_chunk = max(k for k in range(1, lane_tiles + 1) if lane_tiles % k == 0 and 2 * k <= n_sup)
        n_shards = 2 * n_chunk
        width = chan * pix // n_chunk
        dims = (n_tgt, n_sup, n_shards, n_chunk, width, side)
        half = nt // 2
        pad_rows = (side // SUBL) * (side + 2) * SUBL
        shard = (n_shards, half, width)
        dma = pltpu.SemaphoreType.DMA
        sems = []
        for n in (n_tgt, n_sup, n_sup, n_sup, n_sup, n_sup, n_tgt):
            sems += [dma((n - 1,)), dma((n - 1,))]
        f32map = lambda n: pltpu.VMEM((n, pix, LANES), F32)
        scratch = [
            pltpu.VMEM((n_tgt,) + shard, BF16),
            pltpu.VMEM(shard, BF16),
            pltpu.VMEM((n_tgt - 1,) + shard, BF16),
            pltpu.VMEM((n_sup - 1, half, width), BF16),
            pltpu.VMEM(shard, BF16),
            pltpu.VMEM((nt, chan * pix), BF16),
            pltpu.VMEM((n_sup, ns, LANES), F32),
            pltpu.VMEM((n_sup, SUBL, LANES), F32),
            pltpu.VMEM((n_sup, SUBL, n_sup * SUBL), F32),
            pltpu.VMEM((n_sup - 1, SUBL, n_sup * SUBL), F32),
            pltpu.VMEM((n_sup, SUBL, LANES), F32),
            pltpu.VMEM((chan, SUBL, pix), F32),
            pltpu.VMEM((n_tgt - 1, chan, SUBL, pix), F32),
            pltpu.VMEM((chan, SUBL, pix), F32),
            f32map(chan),
            f32map(LAYERS),
            pltpu.VMEM((LAYERS, SUBL, pix), F32),
            f32map(chan),
            f32map(LAYERS),
            f32map(LAYERS),
            f32map(LAYERS),
            f32map(LAYERS + chan),
            pltpu.VMEM((pad_rows, LANES), F32),
            pltpu.VMEM((pad_rows, LANES), F32),
            pltpu.VMEM((pix, LANES), F32),
            pltpu.VMEM(((LAYERS + chan) * SUBL, pix), F32),
            pltpu.VMEM((n_sup * SUBL, LANES), F32),
        ] + sems
        vmem = pl.BlockSpec(memory_space=pltpu.VMEM)
        residual, grad = pl.pallas_call(
            functools.partial(kernel, dims),
            out_shape=(
                jax.ShapeDtypeStruct((nt, per_owner), F32),
                jax.ShapeDtypeStruct((chan, ns, pix), F32),
            ),
            in_specs=[vmem] * 5,
            out_specs=(vmem, vmem),
            scratch_shapes=scratch,
            compiler_params=pltpu.CompilerParams(collective_id=0, has_side_effects=True, vmem_limit_bytes=60000 * 1024),
        )(target_index.reshape(1, -1), labels.reshape(1, nt), image_pool, support.transpose(1, 0, 2), ridge_coef)
        return residual, grad.transpose(1, 0, 2)

    in_specs = (P(("tgt", "sup"), None), P(), P("tgt"), P("sup", None, None), P("sup", None))
    out_specs = (P("tgt", "sup"), P("sup", None, None))
    return jax.shard_map(local, mesh=mesh, in_specs=in_specs, out_specs=out_specs, check_vma=False)
```

```python
import functools
import math

import jax
import jax.numpy as jnp
from jax import lax
from jax.experimental import pallas as pl
from jax.experimental.pallas import tpu as pltpu
from jax.sharding import PartitionSpec as P

LAYERS = 4
HI = lax.Precision.HIGHEST
MESH = pl.DeviceIdType.MESH
F32 = jnp.float32
BF16 = jnp.bfloat16
TWO_PI = 2.0 / math.pi
LANES = 128
SUBL = 8


def arcsin(x):
    a = jnp.abs(x)
    big = a > 0.5
    z = jnp.where(big, 0.5 - 0.5 * a, x * x)
    root = jnp.where(big, z * lax.rsqrt(jnp.maximum(z, 1e-30)), a)
    p = 4.2163199048e-2 * z + 2.4181311049e-2
    p = p * z + 4.5470025998e-2
    p = p * z + 7.4953002686e-2
    p = p * z + 1.6666752422e-1
    p = p * (z * root) + root
    r = jnp.where(big, 0.5 * math.pi - 2.0 * p, p)
    return jnp.where(x < 0.0, -r, r)


def box_rows(x, side):
    pix = x.shape[-1]
    p = lax.broadcasted_iota(jnp.int32, x.shape, 1)
    col = p % side
    row = (
        x
        + jnp.where(col > 0, pltpu.roll(x, 1, 1), 0.0)
        + jnp.where(col < side - 1, pltpu.roll(x, pix - 1, 1), 0.0)
    )
    return (
        row
        + jnp.where(p >= side, pltpu.roll(row, side, 1), 0.0)
        + jnp.where(p < pix - side, pltpu.roll(row, pix - side, 1), 0.0)
    )


def self_vars(self0, side):
    act, out = self0, []
    for depth in range(LAYERS):
        var = (2.0 / 9.0) * box_rows(act, side) + 0.1
        out.append(var)
        if depth < LAYERS - 1:
            act = TWO_PI * arcsin(2.0 * var / (1.0 + 2.0 * var))
    return out


def dot0(a, b, precision=None):
    return lax.dot_general(
        a, b, (((0,), (0,)), ((), ())), precision=precision, preferred_element_type=F32
    )


def split3(x):
    hi = x.astype(BF16)
    rest = x - hi.astype(F32)
    mid = rest.astype(BF16)
    low = (rest - mid.astype(F32)).astype(BF16)
    return hi, mid, low


def kernel(
    dims, idx_ref, lab_ref, pool_ref, sup_ref, ridge_ref, res_ref, grad_ref,
    psend, pown, prec, rsbuf, tbuf, tfull, rcls, rown, psrc, pdst, kbuf, gsend, grecv,
    s8, sexp, rbexp, svar, texp, wbuf, a1, a2, hs, pad_a, pad_b, usum, ut, coef,
    p_s, p_r, rs_s, rs_r, ag_s, ag_r, r_s, r_r, q_s, q_r, k_s, k_r, g_s, g_r,
):
    n_tgt, n_sup, n_shards, n_chunk, width, side = dims
    chan, ns, pix = sup_ref.shape
    nt = res_ref.shape[0]
    pool_rows = pool_ref.shape[0]
    classes = ridge_ref.shape[1]
    per_owner = res_ref.shape[1]
    qn = side // SUBL
    mtile = pix // SUBL
    stride_q = (side + 2) * SUBL
    me = lax.axis_index("sup")
    grp = lax.axis_index("tgt")
    half = nt // 2

    barrier = pltpu.get_barrier_semaphore()
    for d in range(1, n_sup):
        pl.semaphore_signal(barrier, inc=1, device_id=(grp, lax.rem(me + d, n_sup)), device_id_type=MESH)
    for d in range(1, n_tgt):
        pl.semaphore_signal(barrier, inc=1, device_id=(lax.rem(grp + d, n_tgt), me), device_id_type=MESH)

    base = (grp * n_sup + me) * pool_rows
    ids = idx_ref[...] - base
    row_id = lax.broadcasted_iota(jnp.int32, (pool_rows, n_tgt * nt), 0)
    selector = (row_id == ids).astype(F32).astype(BF16)
    for ch in range(n_chunk):
        block = dot0(selector, pool_ref[:, ch * width:(ch + 1) * width]).astype(BF16)
        for g in range(n_tgt):
            for h in range(2):
                psend[g, h * n_chunk + ch] = block[g * nt + h * half:g * nt + (h + 1) * half]
    pl.semaphore_wait(barrier, n_sup + n_tgt - 2)

    def class_tile(k):
        return pl.ds(pl.multiple_of(((k * per_owner) // LANES) * LANES, LANES), LANES)

    def ridge_copy(d):
        peer = lax.rem(me + d, n_sup)
        return pltpu.make_async_remote_copy(
            src_ref=ridge_ref.at[:, class_tile(peer)], dst_ref=rcls.at[me],
            send_sem=r_s.at[d - 1], recv_sem=r_r.at[d - 1],
            device_id=(grp, peer), device_id_type=MESH,
        )

    def tgt_copy(d):
        return pltpu.make_async_remote_copy(
            src_ref=psend.at[lax.rem(grp + d, n_tgt)], dst_ref=prec.at[d - 1],
            send_sem=p_s.at[d - 1], recv_sem=p_r.at[d - 1],
            device_id=(lax.rem(grp + d, n_tgt), me), device_id_type=MESH,
        )

    for d in range(1, n_tgt):
        tgt_copy(d).start()
    for d in range(1, n_sup):
        ridge_copy(d).start()
    rcls[me] = ridge_ref[:, class_tile(me)]
    for d in range(1, n_tgt):
        tgt_copy(d).wait_recv()
    total = psend[grp]
    for d in range(1, n_tgt):
        total = total + prec[d - 1]
    pown[...] = total

    def rs_copy(d):
        peer = lax.rem(me + d, n_sup)
        return peer, pltpu.make_async_remote_copy(
            src_ref=pown.at[lax.rem(peer, n_shards)], dst_ref=rsbuf.at[d - 1],
            send_sem=rs_s.at[d - 1], recv_sem=rs_r.at[d - 1],
            device_id=(grp, peer), device_id_type=MESH,
        )

    def when(cond, fn):
        if n_shards == n_sup:
            fn()
        else:
            pl.when(cond)(fn)

    for d in range(1, n_sup):
        peer, copy = rs_copy(d)
        when(peer < n_shards, copy.start)

    for c in range(chan):
        s8[c, ns:, :] = jnp.zeros((SUBL - ns, pix), F32)
        s8[c, :ns, :] = sup_ref[c]
    sup_self = s8[0] * s8[0]
    for c in range(1, chan):
        sup_self = sup_self + s8[c] * s8[c]
    svs = self_vars(sup_self / chan, side)
    row8 = lax.broadcasted_iota(jnp.int32, (SUBL, LANES), 0)
    lane8 = lax.broadcasted_iota(jnp.int32, (SUBL, LANES), 1)
    hot_j = (row8 == lane8 // nt).astype(F32)
    for depth in range(LAYERS):
        svar[depth] = svs[depth]
    def stacked(x):
        return jnp.concatenate([y.astype(F32) for y in split3(x)], axis=0).astype(BF16)

    hot_j3 = jnp.concatenate([hot_j] * 3, axis=0).astype(BF16)
    for c in range(chan):
        parts = stacked(s8[c])
        for s in range(SUBL):
            cut = slice(s * mtile, (s + 1) * mtile)
            sexp[c, cut, :] = dot0(parts[:, cut], hot_j3)
    for depth in range(LAYERS):
        parts = stacked(lax.rsqrt(1.0 + 2.0 * svs[depth]))
        for s in range(SUBL):
            cut = slice(s * mtile, (s + 1) * mtile)
            rbexp[depth, cut, :] = dot0(parts[:, cut], hot_j3)
    zero_tile = jnp.zeros((SUBL, LANES), F32)
    for buf in (pad_a, pad_b):
        for q in range(qn):
            buf[q * stride_q:q * stride_q + SUBL, :] = zero_tile
            buf[(q + 1) * stride_q - SUBL:(q + 1) * stride_q, :] = zero_tile

    def ag_copy(d):
        return pltpu.make_async_remote_copy(
            src_ref=tbuf.at[lax.rem(me, n_shards)], dst_ref=tbuf.at[lax.rem(me, n_shards)],
            send_sem=ag_s.at[d - 1], recv_sem=ag_r.at[d - 1],
            device_id=(grp, lax.rem(me + d, n_sup)), device_id_type=MESH,
        )

    def own_shard():
        acc = pown[me].astype(F32)
        for d in range(1, n_sup):
            rs_copy(d)[1].wait_recv()
            acc = acc + rsbuf[d - 1].astype(F32)
        tbuf[me] = acc.astype(BF16)
        for d in range(1, n_sup):
            ag_copy(d).start()

    when(me < n_shards, own_shard)

    first = me * per_owner
    chunk = (first // LANES) * LANES
    lane_c = lax.broadcasted_iota(jnp.int32, (ns, LANES), 1) + chunk
    own_class = (lane_c >= first) & (lane_c < first + per_owner)
    for d in range(1, n_sup):
        ridge_copy(d).wait_recv()
    for k in range(n_sup):
        rown[k, :ns, :] = jnp.where(own_class, rcls[k], 0.0)
        rown[k, ns:, :] = jnp.zeros((SUBL - ns, LANES), F32)
    rows = rown[...].reshape(n_sup * SUBL, LANES)
    psrc[...] = lax.dot_general(
        rows, rows, (((1,), (1,)), ((), ())), precision=HI, preferred_element_type=F32
    ).reshape(n_sup, SUBL, n_sup * SUBL)

    def gram_copy(d):
        peer = lax.rem(me + d, n_sup)
        return pltpu.make_async_remote_copy(
            src_ref=psrc.at[peer], dst_ref=pdst.at[d - 1],
            send_sem=q_s.at[d - 1], recv_sem=q_r.at[d - 1],
            device_id=(grp, peer), device_id_type=MESH,
        )

    for d in range(1, n_sup):
        gram_copy(d).start()
    row_t = lax.broadcasted_iota(jnp.int32, (nt, LANES), 0)
    lane_t = lax.broadcasted_iota(jnp.int32, (nt, LANES), 1)
    hot_i = (row_t == lane_t % nt).astype(F32).astype(BF16)
    for d in range(1, n_sup):
        when(lax.rem(me - d + n_sup, n_sup) < n_shards, ag_copy(d).wait_recv)

    for h in range(2):
        for ch in range(n_chunk):
            tfull[h * half:(h + 1) * half, ch * width:(ch + 1) * width] = tbuf[h * n_chunk + ch]

    tgt_self = jnp.zeros((nt, pix), F32)
    for c in range(chan):
        t = tfull[:, c * pix:(c + 1) * pix].astype(F32)
        tgt_self = tgt_self + t * t
    tvs = self_vars(tgt_self / chan, side)
    hot_i3 = jnp.concatenate([hot_i] * 3, axis=0)
    for s in range(SUBL):
        cut = slice(s * mtile, (s + 1) * mtile)
        pair0 = jnp.zeros((mtile, LANES), F32)
        for c in range(chan):
            t = dot0(tfull[:, c * pix + s * mtile:c * pix + (s + 1) * mtile], hot_i)
            texp[c, pl.ds(s, mtile, stride=SUBL), :] = t
            pair0 = pair0 + t * sexp[c, cut, :]
        pair0 = pair0 / chan
        for q in range(qn):
            pad_a[pl.ds(q * stride_q + SUBL + s, side, stride=SUBL), :] = pair0[q * side:(q + 1) * side]
        for depth in range(LAYERS):
            inv = lax.rsqrt(1.0 + 2.0 * tvs[depth][:, cut])
            wide = dot0(jnp.concatenate(split3(inv), axis=0), hot_i3)
            wbuf[depth, pl.ds(s, mtile, stride=SUBL), :] = wide * rbexp[depth, cut, :]

    sub = lax.broadcasted_iota(jnp.int32, (SUBL, LANES), 0)

    def box_column(buf, c):
        sums = []
        for q in range(qn):
            def at(k):
                return buf[pl.ds(pl.multiple_of(q * stride_q + (c + k) * SUBL, SUBL), SUBL), :]
            sums.append(at(0) + at(1) + at(2))
        up = jnp.where(sub > 0, pltpu.roll(sums[-1], 1, 0), 0.0)
        down = jnp.where(sub < SUBL - 1, pltpu.roll(sums[0], SUBL - 1, 0), 0.0)
        ext = [up] + sums + [down]
        return [ext[q] + ext[q + 1] + ext[q + 2] for q in range(qn)]

    def tile(q, c):
        return pl.ds(pl.multiple_of((q * side + c) * SUBL, SUBL), SUBL)

    def padded(q, c):
        return pl.ds(pl.multiple_of(q * stride_q + (c + 1) * SUBL, SUBL), SUBL)

    def forward(depth, src, dst):
        def body(c, acc):
            sums = box_column(src, c)
            for q in range(qn):
                w = wbuf[depth, tile(q, c), :]
                ang = (sums[q] * (4.0 / 9.0) + 0.2) * w
                der = TWO_PI * lax.rsqrt(1.0 - ang * ang)
                a1[depth, tile(q, c), :] = der * w
                a2[depth, tile(q, c), :] = der * ang
                pair = TWO_PI * arcsin(ang)
                if dst is None:
                    acc = acc + pair
                else:
                    dst[padded(q, c), :] = pair
            return acc
        return lax.fori_loop(0, side, body, zero_tile, unroll=4)

    bufs = (pad_a, pad_b)
    for depth in range(LAYERS - 1):
        forward(depth, bufs[depth % 2], bufs[(depth + 1) % 2])
    acc = forward(LAYERS - 1, bufs[(LAYERS - 1) % 2], None)
    krow = jnp.sum(acc, axis=0, keepdims=True) / pix
    krows = jnp.broadcast_to(krow, (SUBL, LANES))
    turn = (row8 + SUBL * ns - lane8 // nt) % ns
    ktile = krows
    for d in range(1, ns):
        ktile = jnp.where(turn == d, pltpu.roll(krows, LANES - d * nt, 1), ktile)
    kbuf[me] = ktile

    def k_copy(d):
        return pltpu.make_async_remote_copy(
            src_ref=kbuf.at[me], dst_ref=kbuf.at[me],
            send_sem=k_s.at[d - 1], recv_sem=k_r.at[d - 1],
            device_id=(grp, lax.rem(me + d, n_sup)), device_id_type=MESH,
        )

    for d in range(1, n_sup):
        k_copy(d).start()

    mine = jnp.concatenate([ridge_ref[...], jnp.zeros((SUBL - ns, classes), F32)], axis=0)
    labels = lab_ref[...].astype(F32)
    lab_row = jnp.dot(
        jnp.broadcast_to(labels, (SUBL, nt)), hot_i.astype(F32), precision=HI, preferred_element_type=F32
    )[0:1]
    class_id = lax.broadcasted_iota(jnp.int32, (classes, LANES), 0).astype(F32)
    label_hot = (class_id == lab_row).astype(F32).astype(BF16)
    picked = jnp.dot(stacked(mine), label_hot, preferred_element_type=F32)
    picked = picked[:SUBL] + picked[SUBL:2 * SUBL] + picked[2 * SUBL:]
    lab_term = jnp.sum(picked * hot_j, axis=0, keepdims=True)

    gram = psrc[me]
    for d in range(1, n_sup):
        gram_copy(d).wait_recv()
        gram = gram + pdst[d - 1]
    coef[...] = dot0(gram, hot_j, HI)

    for d in range(1, n_sup):
        k_copy(d).wait_recv()
    kall = kbuf[...].reshape(n_sup * SUBL, LANES)
    kg = jnp.sum(kall * coef[...], axis=0, keepdims=True) - lab_term
    scale = float(side * side) / nt / pix
    top = jnp.broadcast_to(kg * scale, (SUBL, LANES))

    def backward(depth, src, dst):
        def body(c, carry):
            if src is None:
                grads = [top] * qn
            else:
                grads = [x * (4.0 / 9.0) for x in box_column(src, c)]
            for q in range(qn):
                dst[padded(q, c), :] = grads[q] * a1[depth, tile(q, c), :]
                hs[depth, tile(q, c), :] = grads[q] * a2[depth, tile(q, c), :]
            return carry
        lax.fori_loop(0, side, body, 0, unroll=4)

    src = None
    for step, depth in enumerate(reversed(range(LAYERS))):
        backward(depth, src, bufs[step % 2])
        src = bufs[step % 2]

    def input_grad(c, carry):
        grads = [x * (4.0 / 9.0 / chan) for x in box_column(src, c)]
        for q in range(qn):
            for ch in range(chan):
                hs[LAYERS + ch, tile(q, c), :] = grads[q] * texp[ch, tile(q, c), :]
        return carry
    lax.fori_loop(0, side, input_grad, 0, unroll=4)

    row_l = lax.broadcasted_iota(jnp.int32, (LANES, LANES), 0)
    col_l = lax.broadcasted_iota(jnp.int32, (LANES, LANES), 1)
    gather = [
        (col_l == a * SUBL + row_l // nt).astype(F32).astype(BF16) for a in range(LAYERS + chan)
    ]
    gather = [jnp.concatenate([x, x], axis=0) for x in gather]
    blk = 256
    for b in range(pix // blk):
        total = jnp.zeros((blk, LANES), F32)
        for a in range(LAYERS + chan):
            x = hs[a, b * blk:(b + 1) * blk, :]
            hi = x.astype(BF16)
            low = (x - hi.astype(F32)).astype(BF16)
            total = total + jnp.dot(
                jnp.concatenate([hi, low], axis=1), gather[a], preferred_element_type=F32
            )
        usum[b * blk:(b + 1) * blk, :] = total
    for s in range(SUBL):
        turned = usum[pl.ds(s, mtile, stride=SUBL), :].T
        ut[:, s * mtile:(s + 1) * mtile] = turned[:(LAYERS + chan) * SUBL]

    dact = None
    for depth in reversed(range(LAYERS)):
        var = svar[depth]
        dvar = -ut[depth * SUBL:(depth + 1) * SUBL, :] / (1.0 + 2.0 * var)
        if dact is not None:
            dvar = dvar + dact * (2.0 * TWO_PI) * lax.rsqrt(1.0 + 4.0 * var) / (1.0 + 2.0 * var)
        dact = (2.0 / 9.0) * box_rows(dvar, side)
    for c in range(chan):
        a = LAYERS + c
        gsend[c] = ut[a * SUBL:(a + 1) * SUBL, :] + dact * (2.0 / chan) * s8[c]

    def g_copy(d):
        return pltpu.make_async_remote_copy(
            src_ref=gsend, dst_ref=grecv.at[d - 1],
            send_sem=g_s.at[d - 1], recv_sem=g_r.at[d - 1],
            device_id=(lax.rem(grp + d, n_tgt), me), device_id_type=MESH,
        )

    for d in range(1, n_tgt):
        g_copy(d).start()

    pred = dot0(kall[:, :nt], rows, HI)
    lab_col = jnp.sum(jnp.where(row_t == lane_t, lab_row, 0.0), axis=1, keepdims=True)
    pred = pred - ((lane_t + chunk).astype(F32) == lab_col).astype(F32)
    pred = pltpu.roll(pred, lax.rem(LANES - first % LANES, LANES), 1)
    res_ref[...] = pred[:, :per_owner]

    for d in range(1, n_tgt):
        g_copy(d).wait_recv()
    for c in range(chan):
        terms = gsend[c]
        if n_tgt == 2:
            terms = terms + grecv[0, c]
        else:
            terms = jnp.zeros_like(terms)
            for g in range(n_tgt):
                dist = lax.rem(grp - g + n_tgt, n_tgt)
                part = grecv[jnp.maximum(dist - 1, 0), c]
                terms = terms + jnp.where(dist == 0, gsend[c], part)
        grad_ref[c] = terms[:ns]

    for d in range(1, n_tgt):
        tgt_copy(d).wait_send()
        g_copy(d).wait_send()
    for d in range(1, n_sup):
        peer, copy = rs_copy(d)
        when(peer < n_shards, copy.wait_send)
        when(me < n_shards, ag_copy(d).wait_send)
        ridge_copy(d).wait_send()
        gram_copy(d).wait_send()
        k_copy(d).wait_send()


def solution(mesh):
    n_tgt, n_sup = mesh.shape["tgt"], mesh.shape["sup"]

    def local(image_pool, target_index, labels, support, ridge_coef):
        nt = labels.shape[0]
        ns, chan, pix = support.shape
        side = math.isqrt(pix)
        classes = ridge_coef.shape[1]
        per_owner = classes // n_sup
        lane_tiles = chan * pix // LANES
        n_chunk = max(k for k in range(1, lane_tiles + 1) if lane_tiles % k == 0 and 2 * k <= n_sup)
        n_shards = 2 * n_chunk
        width = chan * pix // n_chunk
        dims = (n_tgt, n_sup, n_shards, n_chunk, width, side)
        half = nt // 2
        pad_rows = (side // SUBL) * (side + 2) * SUBL
        shard = (n_shards, half, width)
        dma = pltpu.SemaphoreType.DMA
        sems = []
        for n in (n_tgt, n_sup, n_sup, n_sup, n_sup, n_sup, n_tgt):
            sems += [dma((n - 1,)), dma((n - 1,))]
        f32map = lambda n: pltpu.VMEM((n, pix, LANES), F32)
        scratch = [
            pltpu.VMEM((n_tgt,) + shard, BF16),
            pltpu.VMEM(shard, BF16),
            pltpu.VMEM((n_tgt - 1,) + shard, BF16),
            pltpu.VMEM((n_sup - 1, half, width), BF16),
            pltpu.VMEM(shard, BF16),
            pltpu.VMEM((nt, chan * pix), BF16),
            pltpu.VMEM((n_sup, ns, LANES), F32),
            pltpu.VMEM((n_sup, SUBL, LANES), F32),
            pltpu.VMEM((n_sup, SUBL, n_sup * SUBL), F32),
            pltpu.VMEM((n_sup - 1, SUBL, n_sup * SUBL), F32),
            pltpu.VMEM((n_sup, SUBL, LANES), F32),
            pltpu.VMEM((chan, SUBL, pix), F32),
            pltpu.VMEM((n_tgt - 1, chan, SUBL, pix), F32),
            pltpu.VMEM((chan, SUBL, pix), F32),
            f32map(chan),
            f32map(LAYERS),
            pltpu.VMEM((LAYERS, SUBL, pix), F32),
            f32map(chan),
            f32map(LAYERS),
            f32map(LAYERS),
            f32map(LAYERS),
            f32map(LAYERS + chan),
            pltpu.VMEM((pad_rows, LANES), F32),
            pltpu.VMEM((pad_rows, LANES), F32),
            pltpu.VMEM((pix, LANES), F32),
            pltpu.VMEM(((LAYERS + chan) * SUBL, pix), F32),
            pltpu.VMEM((n_sup * SUBL, LANES), F32),
        ] + sems
        vmem = pl.BlockSpec(memory_space=pltpu.VMEM)
        residual, grad = pl.pallas_call(
            functools.partial(kernel, dims),
            out_shape=(
                jax.ShapeDtypeStruct((nt, per_owner), F32),
                jax.ShapeDtypeStruct((chan, ns, pix), F32),
            ),
            in_specs=[vmem] * 5,
            out_specs=(vmem, vmem),
            scratch_shapes=scratch,
            compiler_params=pltpu.CompilerParams(collective_id=0, has_side_effects=True, vmem_limit_bytes=60000 * 1024),
        )(target_index.reshape(1, -1), labels.reshape(1, nt), image_pool, support.transpose(1, 0, 2), ridge_coef)
        return residual, grad.transpose(1, 0, 2)

    in_specs = (P(("tgt", "sup"), None), P(), P("tgt"), P("sup", None, None), P("sup", None))
    out_specs = (P("tgt", "sup"), P("sup", None, None))
    return jax.shard_map(local, mesh=mesh, in_specs=in_specs, out_specs=out_specs, check_vma=False)
```

```python
import functools
import math

import jax
import jax.numpy as jnp
from jax import lax
from jax.experimental import pallas as pl
from jax.experimental.pallas import tpu as pltpu
from jax.sharding import PartitionSpec as P

LAYERS = 4
HI = lax.Precision.HIGHEST
MESH = pl.DeviceIdType.MESH
F32 = jnp.float32
BF16 = jnp.bfloat16
TWO_PI = 2.0 / math.pi
LANES = 128
SUBL = 8


def arcsin(x):
    a = jnp.abs(x)
    big = a > 0.5
    z = jnp.where(big, 0.5 - 0.5 * a, x * x)
    root = jnp.where(big, z * lax.rsqrt(jnp.maximum(z, 1e-30)), a)
    p = 4.2163199048e-2 * z + 2.4181311049e-2
    p = p * z + 4.5470025998e-2
    p = p * z + 7.4953002686e-2
    p = p * z + 1.6666752422e-1
    p = p * (z * root) + root
    r = jnp.where(big, 0.5 * math.pi - 2.0 * p, p)
    return jnp.where(x < 0.0, -r, r)


def box_rows(x, side):
    pix = x.shape[-1]
    p = lax.broadcasted_iota(jnp.int32, x.shape, 1)
    col = p % side
    row = (
        x
        + jnp.where(col > 0, pltpu.roll(x, 1, 1), 0.0)
        + jnp.where(col < side - 1, pltpu.roll(x, pix - 1, 1), 0.0)
    )
    return (
        row
        + jnp.where(p >= side, pltpu.roll(row, side, 1), 0.0)
        + jnp.where(p < pix - side, pltpu.roll(row, pix - side, 1), 0.0)
    )


def self_vars(self0, side):
    act, out = self0, []
    for depth in range(LAYERS):
        var = (2.0 / 9.0) * box_rows(act, side) + 0.1
        out.append(var)
        if depth < LAYERS - 1:
            act = TWO_PI * arcsin(2.0 * var / (1.0 + 2.0 * var))
    return out


def dot0(a, b, precision=None):
    return lax.dot_general(
        a, b, (((0,), (0,)), ((), ())), precision=precision, preferred_element_type=F32
    )


def split3(x):
    hi = x.astype(BF16)
    rest = x - hi.astype(F32)
    mid = rest.astype(BF16)
    low = (rest - mid.astype(F32)).astype(BF16)
    return hi, mid, low


def kernel(
    dims, idx_ref, lab_ref, pool_ref, sup_ref, ridge_ref, res_ref, grad_ref,
    psend, pown, prec, rsbuf, tbuf, tfull, rcls, rown, psrc, pdst, kbuf, gsend, grecv,
    s8, sexp, rbexp, svar, texp, wbuf, a1, a2, hs, pad_a, pad_b, usum, ut, coef,
    p_s, p_r, rs_s, rs_r, ag_s, ag_r, r_s, r_r, q_s, q_r, k_s, k_r, g_s, g_r,
):
    n_tgt, n_sup, n_shards, n_chunk, width, side = dims
    chan, ns, pix = sup_ref.shape
    nt = res_ref.shape[0]
    pool_rows = pool_ref.shape[0]
    classes = ridge_ref.shape[1]
    per_owner = res_ref.shape[1]
    qn = side // SUBL
    mtile = pix // SUBL
    stride_q = (side + 2) * SUBL
    me = lax.axis_index("sup")
    grp = lax.axis_index("tgt")
    half = nt // 2

    barrier = pltpu.get_barrier_semaphore()
    for d in range(1, n_sup):
        pl.semaphore_signal(barrier, inc=1, device_id=(grp, lax.rem(me + d, n_sup)), device_id_type=MESH)
    for d in range(1, n_tgt):
        pl.semaphore_signal(barrier, inc=1, device_id=(lax.rem(grp + d, n_tgt), me), device_id_type=MESH)

    base = (grp * n_sup + me) * pool_rows
    ids = idx_ref[...] - base
    row_id = lax.broadcasted_iota(jnp.int32, (pool_rows, n_tgt * nt), 0)
    selector = (row_id == ids).astype(F32).astype(BF16)
    for ch in range(n_chunk):
        block = dot0(selector, pool_ref[:, ch * width:(ch + 1) * width]).astype(BF16)
        for g in range(n_tgt):
            for h in range(2):
                psend[g, h * n_chunk + ch] = block[g * nt + h * half:g * nt + (h + 1) * half]
    pl.semaphore_wait(barrier, n_sup + n_tgt - 2)

    def class_tile(k):
        return pl.ds(pl.multiple_of(((k * per_owner) // LANES) * LANES, LANES), LANES)

    def ridge_copy(d):
        peer = lax.rem(me + d, n_sup)
        return pltpu.make_async_remote_copy(
            src_ref=ridge_ref.at[:, class_tile(peer)], dst_ref=rcls.at[me],
            send_sem=r_s.at[d - 1], recv_sem=r_r.at[d - 1],
            device_id=(grp, peer), device_id_type=MESH,
        )

    def tgt_copy(d):
        return pltpu.make_async_remote_copy(
            src_ref=psend.at[lax.rem(grp + d, n_tgt)], dst_ref=prec.at[d - 1],
            send_sem=p_s.at[d - 1], recv_sem=p_r.at[d - 1],
            device_id=(lax.rem(grp + d, n_tgt), me), device_id_type=MESH,
        )

    for d in range(1, n_tgt):
        tgt_copy(d).start()
    for d in range(1, n_sup):
        ridge_copy(d).start()
    rcls[me] = ridge_ref[:, class_tile(me)]
    for d in range(1, n_tgt):
        tgt_copy(d).wait_recv()
    total = psend[grp]
    for d in range(1, n_tgt):
        total = total + prec[d - 1]
    pown[...] = total

    def rs_copy(d):
        peer = lax.rem(me + d, n_sup)
        return peer, pltpu.make_async_remote_copy(
            src_ref=pown.at[lax.rem(peer, n_shards)], dst_ref=rsbuf.at[d - 1],
            send_sem=rs_s.at[d - 1], recv_sem=rs_r.at[d - 1],
            device_id=(grp, peer), device_id_type=MESH,
        )

    def when(cond, fn):
        if n_shards == n_sup:
            fn()
        else:
            pl.when(cond)(fn)

    for d in range(1, n_sup):
        peer, copy = rs_copy(d)
        when(peer < n_shards, copy.start)

    for c in range(chan):
        s8[c, ns:, :] = jnp.zeros((SUBL - ns, pix), F32)
        s8[c, :ns, :] = sup_ref[c]
    sup_self = s8[0] * s8[0]
    for c in range(1, chan):
        sup_self = sup_self + s8[c] * s8[c]
    svs = self_vars(sup_self / chan, side)
    row8 = lax.broadcasted_iota(jnp.int32, (SUBL, LANES), 0)
    lane8 = lax.broadcasted_iota(jnp.int32, (SUBL, LANES), 1)
    hot_j = (row8 == lane8 // nt).astype(F32)
    for depth in range(LAYERS):
        svar[depth] = svs[depth]
    def stacked(x):
        return jnp.concatenate([y.astype(F32) for y in split3(x)], axis=0).astype(BF16)

    hot_j3 = jnp.concatenate([hot_j] * 3, axis=0).astype(BF16)
    for c in range(chan):
        parts = stacked(s8[c])
        for s in range(SUBL):
            cut = slice(s * mtile, (s + 1) * mtile)
            sexp[c, cut, :] = dot0(parts[:, cut], hot_j3)
    for depth in range(LAYERS):
        parts = stacked(lax.rsqrt(1.0 + 2.0 * svs[depth]))
        for s in range(SUBL):
            cut = slice(s * mtile, (s + 1) * mtile)
            rbexp[depth, cut, :] = dot0(parts[:, cut], hot_j3)
    zero_tile = jnp.zeros((SUBL, LANES), F32)
    for buf in (pad_a, pad_b):
        for q in range(qn):
            buf[q * stride_q:q * stride_q + SUBL, :] = zero_tile
            buf[(q + 1) * stride_q - SUBL:(q + 1) * stride_q, :] = zero_tile

    def ag_copy(d):
        return pltpu.make_async_remote_copy(
            src_ref=tbuf.at[lax.rem(me, n_shards)], dst_ref=tbuf.at[lax.rem(me, n_shards)],
            send_sem=ag_s.at[d - 1], recv_sem=ag_r.at[d - 1],
            device_id=(grp, lax.rem(me + d, n_sup)), device_id_type=MESH,
        )

    def own_shard():
        acc = pown[me].astype(F32)
        for d in range(1, n_sup):
            rs_copy(d)[1].wait_recv()
            acc = acc + rsbuf[d - 1].astype(F32)
        tbuf[me] = acc.astype(BF16)
        for d in range(1, n_sup):
            ag_copy(d).start()

    when(me < n_shards, own_shard)

    first = me * per_owner
    chunk = (first // LANES) * LANES
    lane_c = lax.broadcasted_iota(jnp.int32, (ns, LANES), 1) + chunk
    own_class = (lane_c >= first) & (lane_c < first + per_owner)
    for d in range(1, n_sup):
        ridge_copy(d).wait_recv()
    for k in range(n_sup):
        rown[k, :ns, :] = jnp.where(own_class, rcls[k], 0.0)
        rown[k, ns:, :] = jnp.zeros((SUBL - ns, LANES), F32)
    rows = rown[...].reshape(n_sup * SUBL, LANES)
    psrc[...] = lax.dot_general(
        rows, rows, (((1,), (1,)), ((), ())), precision=HI, preferred_element_type=F32
    ).reshape(n_sup, SUBL, n_sup * SUBL)

    def gram_copy(d):
        peer = lax.rem(me + d, n_sup)
        return pltpu.make_async_remote_copy(
            src_ref=psrc.at[peer], dst_ref=pdst.at[d - 1],
            send_sem=q_s.at[d - 1], recv_sem=q_r.at[d - 1],
            device_id=(grp, peer), device_id_type=MESH,
        )

    for d in range(1, n_sup):
        gram_copy(d).start()
    row_t = lax.broadcasted_iota(jnp.int32, (nt, LANES), 0)
    lane_t = lax.broadcasted_iota(jnp.int32, (nt, LANES), 1)
    hot_i = (row_t == lane_t % nt).astype(F32).astype(BF16)
    for d in range(1, n_sup):
        when(lax.rem(me - d + n_sup, n_sup) < n_shards, ag_copy(d).wait_recv)

    for h in range(2):
        for ch in range(n_chunk):
            tfull[h * half:(h + 1) * half, ch * width:(ch + 1) * width] = tbuf[h * n_chunk + ch]

    tgt_self = jnp.zeros((nt, pix), F32)
    for c in range(chan):
        t = tfull[:, c * pix:(c + 1) * pix].astype(F32)
        tgt_self = tgt_self + t * t
    tvs = self_vars(tgt_self / chan, side)
    hot_i3 = jnp.concatenate([hot_i] * 3, axis=0)
    for s in range(SUBL):
        cut = slice(s * mtile, (s + 1) * mtile)
        pair0 = jnp.zeros((mtile, LANES), F32)
        for c in range(chan):
            t = dot0(tfull[:, c * pix + s * mtile:c * pix + (s + 1) * mtile], hot_i)
            texp[c, pl.ds(s, mtile, stride=SUBL), :] = t
            pair0 = pair0 + t * sexp[c, cut, :]
        pair0 = pair0 / chan
        for q in range(qn):
            pad_a[pl.ds(q * stride_q + SUBL + s, side, stride=SUBL), :] = pair0[q * side:(q + 1) * side]
        for depth in range(LAYERS):
            inv = lax.rsqrt(1.0 + 2.0 * tvs[depth][:, cut])
            wide = dot0(jnp.concatenate(split3(inv), axis=0), hot_i3)
            wbuf[depth, pl.ds(s, mtile, stride=SUBL), :] = wide * rbexp[depth, cut, :]

    sub = lax.broadcasted_iota(jnp.int32, (SUBL, LANES), 0)

    def box_column(buf, c):
        sums = []
        for q in range(qn):
            def at(k):
                return buf[pl.ds(pl.multiple_of(q * stride_q + (c + k) * SUBL, SUBL), SUBL), :]
            sums.append(at(0) + at(1) + at(2))
        up = jnp.where(sub > 0, pltpu.roll(sums[-1], 1, 0), 0.0)
        down = jnp.where(sub < SUBL - 1, pltpu.roll(sums[0], SUBL - 1, 0), 0.0)
        ext = [up] + sums + [down]
        return [ext[q] + ext[q + 1] + ext[q + 2] for q in range(qn)]

    def tile(q, c):
        return pl.ds(pl.multiple_of((q * side + c) * SUBL, SUBL), SUBL)

    def padded(q, c):
        return pl.ds(pl.multiple_of(q * stride_q + (c + 1) * SUBL, SUBL), SUBL)

    def forward(depth, src, dst):
        def body(c, acc):
            sums = box_column(src, c)
            for q in range(qn):
                w = wbuf[depth, tile(q, c), :]
                ang = (sums[q] * (4.0 / 9.0) + 0.2) * w
                der = TWO_PI * lax.rsqrt(1.0 - ang * ang)
                a1[depth, tile(q, c), :] = der * w
                a2[depth, tile(q, c), :] = der * ang
                pair = TWO_PI * arcsin(ang)
                if dst is None:
                    acc = acc + pair
                else:
                    dst[padded(q, c), :] = pair
            return acc
        return lax.fori_loop(0, side, body, zero_tile, unroll=4)

    bufs = (pad_a, pad_b)
    for depth in range(LAYERS - 1):
        forward(depth, bufs[depth % 2], bufs[(depth + 1) % 2])
    acc = forward(LAYERS - 1, bufs[(LAYERS - 1) % 2], None)
    krow = jnp.sum(acc, axis=0, keepdims=True) / pix
    kbuf[me] = krow

    def k_copy(d):
        return pltpu.make_async_remote_copy(
            src_ref=kbuf.at[me], dst_ref=kbuf.at[me],
            send_sem=k_s.at[d - 1], recv_sem=k_r.at[d - 1],
            device_id=(grp, lax.rem(me + d, n_sup)), device_id_type=MESH,
        )

    for d in range(1, n_sup):
        k_copy(d).start()

    mine = jnp.concatenate([ridge_ref[...], jnp.zeros((SUBL - ns, classes), F32)], axis=0)
    labels = lab_ref[...].astype(F32)
    lab_row = jnp.dot(
        jnp.broadcast_to(labels, (SUBL, nt)), hot_i.astype(F32), precision=HI, preferred_element_type=F32
    )[0:1]
    class_id = lax.broadcasted_iota(jnp.int32, (classes, LANES), 0).astype(F32)
    label_hot = (class_id == lab_row).astype(F32).astype(BF16)
    picked = jnp.dot(stacked(mine), label_hot, preferred_element_type=F32)
    picked = picked[:SUBL] + picked[SUBL:2 * SUBL] + picked[2 * SUBL:]
    lab_term = jnp.sum(picked * hot_j, axis=0, keepdims=True)

    gram = psrc[me]
    for d in range(1, n_sup):
        gram_copy(d).wait_recv()
        gram = gram + pdst[d - 1]
    coef[...] = dot0(gram, hot_j, HI)

    for d in range(1, n_sup):
        k_copy(d).wait_recv()
    krows = jnp.broadcast_to(kbuf[...], (n_sup, SUBL, LANES))
    turn = ((row8 + SUBL * ns - lane8 // nt) % ns)[None]
    kall = krows
    for d in range(1, ns):
        kall = jnp.where(turn == d, pltpu.roll(krows, LANES - d * nt, 2), kall)
    kall = kall.reshape(n_sup * SUBL, LANES)
    kg = jnp.sum(kall * coef[...], axis=0, keepdims=True) - lab_term
    scale = float(side * side) / nt / pix
    top = jnp.broadcast_to(kg * scale, (SUBL, LANES))

    def backward(depth, src, dst):
        def body(c, carry):
            if src is None:
                grads = [top] * qn
            else:
                grads = [x * (4.0 / 9.0) for x in box_column(src, c)]
            for q in range(qn):
                dst[padded(q, c), :] = grads[q] * a1[depth, tile(q, c), :]
                hs[depth, tile(q, c), :] = grads[q] * a2[depth, tile(q, c), :]
            return carry
        lax.fori_loop(0, side, body, 0, unroll=4)

    src = None
    for step, depth in enumerate(reversed(range(LAYERS))):
        backward(depth, src, bufs[step % 2])
        src = bufs[step % 2]

    def input_grad(c, carry):
        grads = [x * (4.0 / 9.0 / chan) for x in box_column(src, c)]
        for q in range(qn):
            for ch in range(chan):
                hs[LAYERS + ch, tile(q, c), :] = grads[q] * texp[ch, tile(q, c), :]
        return carry
    lax.fori_loop(0, side, input_grad, 0, unroll=4)

    row_l = lax.broadcasted_iota(jnp.int32, (LANES, LANES), 0)
    col_l = lax.broadcasted_iota(jnp.int32, (LANES, LANES), 1)
    gather = [
        (col_l == a * SUBL + row_l // nt).astype(F32).astype(BF16) for a in range(LAYERS + chan)
    ]
    gather = [jnp.concatenate([x, x], axis=0) for x in gather]
    blk = 256
    for b in range(pix // blk):
        total = jnp.zeros((blk, LANES), F32)
        for a in range(LAYERS + chan):
            x = hs[a, b * blk:(b + 1) * blk, :]
            hi = x.astype(BF16)
            low = (x - hi.astype(F32)).astype(BF16)
            total = total + jnp.dot(
                jnp.concatenate([hi, low], axis=1), gather[a], preferred_element_type=F32
            )
        usum[b * blk:(b + 1) * blk, :] = total
    for s in range(SUBL):
        turned = usum[pl.ds(s, mtile, stride=SUBL), :].T
        ut[:, s * mtile:(s + 1) * mtile] = turned[:(LAYERS + chan) * SUBL]

    dact = None
    for depth in reversed(range(LAYERS)):
        var = svar[depth]
        dvar = -ut[depth * SUBL:(depth + 1) * SUBL, :] / (1.0 + 2.0 * var)
        if dact is not None:
            dvar = dvar + dact * (2.0 * TWO_PI) * lax.rsqrt(1.0 + 4.0 * var) / (1.0 + 2.0 * var)
        dact = (2.0 / 9.0) * box_rows(dvar, side)
    for c in range(chan):
        a = LAYERS + c
        gsend[c] = ut[a * SUBL:(a + 1) * SUBL, :] + dact * (2.0 / chan) * s8[c]

    def g_copy(d):
        return pltpu.make_async_remote_copy(
            src_ref=gsend, dst_ref=grecv.at[d - 1],
            send_sem=g_s.at[d - 1], recv_sem=g_r.at[d - 1],
            device_id=(lax.rem(grp + d, n_tgt), me), device_id_type=MESH,
        )

    for d in range(1, n_tgt):
        g_copy(d).start()

    pred = dot0(kall[:, :nt], rows, HI)
    lab_col = jnp.sum(jnp.where(row_t == lane_t, lab_row, 0.0), axis=1, keepdims=True)
    pred = pred - ((lane_t + chunk).astype(F32) == lab_col).astype(F32)
    pred = pltpu.roll(pred, lax.rem(LANES - first % LANES, LANES), 1)
    res_ref[...] = pred[:, :per_owner]

    for d in range(1, n_tgt):
        g_copy(d).wait_recv()
    for c in range(chan):
        terms = gsend[c]
        if n_tgt == 2:
            terms = terms + grecv[0, c]
        else:
            terms = jnp.zeros_like(terms)
            for g in range(n_tgt):
                dist = lax.rem(grp - g + n_tgt, n_tgt)
                part = grecv[jnp.maximum(dist - 1, 0), c]
                terms = terms + jnp.where(dist == 0, gsend[c], part)
        grad_ref[c] = terms[:ns]

    for d in range(1, n_tgt):
        tgt_copy(d).wait_send()
        g_copy(d).wait_send()
    for d in range(1, n_sup):
        peer, copy = rs_copy(d)
        when(peer < n_shards, copy.wait_send)
        when(me < n_shards, ag_copy(d).wait_send)
        ridge_copy(d).wait_send()
        gram_copy(d).wait_send()
        k_copy(d).wait_send()


def solution(mesh):
    n_tgt, n_sup = mesh.shape["tgt"], mesh.shape["sup"]

    def local(image_pool, target_index, labels, support, ridge_coef):
        nt = labels.shape[0]
        ns, chan, pix = support.shape
        side = math.isqrt(pix)
        classes = ridge_coef.shape[1]
        per_owner = classes // n_sup
        lane_tiles = chan * pix // LANES
        n_chunk = max(k for k in range(1, lane_tiles + 1) if lane_tiles % k == 0 and 2 * k <= n_sup)
        n_shards = 2 * n_chunk
        width = chan * pix // n_chunk
        dims = (n_tgt, n_sup, n_shards, n_chunk, width, side)
        half = nt // 2
        pad_rows = (side // SUBL) * (side + 2) * SUBL
        shard = (n_shards, half, width)
        dma = pltpu.SemaphoreType.DMA
        sems = []
        for n in (n_tgt, n_sup, n_sup, n_sup, n_sup, n_sup, n_tgt):
            sems += [dma((n - 1,)), dma((n - 1,))]
        f32map = lambda n: pltpu.VMEM((n, pix, LANES), F32)
        scratch = [
            pltpu.VMEM((n_tgt,) + shard, BF16),
            pltpu.VMEM(shard, BF16),
            pltpu.VMEM((n_tgt - 1,) + shard, BF16),
            pltpu.VMEM((n_sup - 1, half, width), BF16),
            pltpu.VMEM(shard, BF16),
            pltpu.VMEM((nt, chan * pix), BF16),
            pltpu.VMEM((n_sup, ns, LANES), F32),
            pltpu.VMEM((n_sup, SUBL, LANES), F32),
            pltpu.VMEM((n_sup, SUBL, n_sup * SUBL), F32),
            pltpu.VMEM((n_sup - 1, SUBL, n_sup * SUBL), F32),
            pltpu.VMEM((n_sup, 1, LANES), F32),
            pltpu.VMEM((chan, SUBL, pix), F32),
            pltpu.VMEM((n_tgt - 1, chan, SUBL, pix), F32),
            pltpu.VMEM((chan, SUBL, pix), F32),
            f32map(chan),
            f32map(LAYERS),
            pltpu.VMEM((LAYERS, SUBL, pix), F32),
            f32map(chan),
            f32map(LAYERS),
            f32map(LAYERS),
            f32map(LAYERS),
            f32map(LAYERS + chan),
            pltpu.VMEM((pad_rows, LANES), F32),
            pltpu.VMEM((pad_rows, LANES), F32),
            pltpu.VMEM((pix, LANES), F32),
            pltpu.VMEM(((LAYERS + chan) * SUBL, pix), F32),
            pltpu.VMEM((n_sup * SUBL, LANES), F32),
        ] + sems
        vmem = pl.BlockSpec(memory_space=pltpu.VMEM)
        residual, grad = pl.pallas_call(
            functools.partial(kernel, dims),
            out_shape=(
                jax.ShapeDtypeStruct((nt, per_owner), F32),
                jax.ShapeDtypeStruct((chan, ns, pix), F32),
            ),
            in_specs=[vmem] * 5,
            out_specs=(vmem, vmem),
            scratch_shapes=scratch,
            compiler_params=pltpu.CompilerParams(collective_id=0, has_side_effects=True, vmem_limit_bytes=60000 * 1024),
        )(target_index.reshape(1, -1), labels.reshape(1, nt), image_pool, support.transpose(1, 0, 2), ridge_coef)
        return residual, grad.transpose(1, 0, 2)

    in_specs = (P(("tgt", "sup"), None), P(), P("tgt"), P("sup", None, None), P("sup", None))
    out_specs = (P("tgt", "sup"), P("sup", None, None))
    return jax.shard_map(local, mesh=mesh, in_specs=in_specs, out_specs=out_specs, check_vma=False)
```

```python
import functools
import math

import jax
import jax.numpy as jnp
from jax import lax
from jax.experimental import pallas as pl
from jax.experimental.pallas import tpu as pltpu
from jax.sharding import PartitionSpec as P

LAYERS = 4
HI = lax.Precision.HIGHEST
MESH = pl.DeviceIdType.MESH
F32 = jnp.float32
BF16 = jnp.bfloat16
TWO_PI = 2.0 / math.pi
LANES = 128
SUBL = 8


def arcsin(x):
    a = jnp.abs(x)
    big = a > 0.5
    z = jnp.where(big, 0.5 - 0.5 * a, x * x)
    root = jnp.where(big, z * lax.rsqrt(jnp.maximum(z, 1e-30)), a)
    p = 4.2163199048e-2 * z + 2.4181311049e-2
    p = p * z + 4.5470025998e-2
    p = p * z + 7.4953002686e-2
    p = p * z + 1.6666752422e-1
    p = p * (z * root) + root
    r = jnp.where(big, 0.5 * math.pi - 2.0 * p, p)
    return jnp.where(x < 0.0, -r, r)


def box_rows(x, side):
    pix = x.shape[-1]
    p = lax.broadcasted_iota(jnp.int32, x.shape, 1)
    col = p % side
    row = (
        x
        + jnp.where(col > 0, pltpu.roll(x, 1, 1), 0.0)
        + jnp.where(col < side - 1, pltpu.roll(x, pix - 1, 1), 0.0)
    )
    return (
        row
        + jnp.where(p >= side, pltpu.roll(row, side, 1), 0.0)
        + jnp.where(p < pix - side, pltpu.roll(row, pix - side, 1), 0.0)
    )


def self_vars(self0, side):
    act, out = self0, []
    for depth in range(LAYERS):
        var = (2.0 / 9.0) * box_rows(act, side) + 0.1
        out.append(var)
        if depth < LAYERS - 1:
            act = TWO_PI * arcsin(2.0 * var / (1.0 + 2.0 * var))
    return out


def dot0(a, b, precision=None):
    return lax.dot_general(
        a, b, (((0,), (0,)), ((), ())), precision=precision, preferred_element_type=F32
    )


def split3(x):
    hi = x.astype(BF16)
    rest = x - hi.astype(F32)
    mid = rest.astype(BF16)
    low = (rest - mid.astype(F32)).astype(BF16)
    return hi, mid, low


def kernel(
    dims, idx_ref, lab_ref, pool_ref, sup_ref, ridge_ref, res_ref, grad_ref,
    psend, pown, prec, rsbuf, tbuf, tfull, rcls, rown, psrc, pdst, kbuf, gsend, grecv,
    s8, sexp, rbexp, svar, texp, wbuf, a1, a2, hs, pad_a, pad_b, usum, ut, coef,
    p_s, p_r, rs_s, rs_r, ag_s, ag_r, r_s, r_r, q_s, q_r, k_s, k_r, g_s, g_r,
):
    n_tgt, n_sup, n_shards, n_chunk, width, side = dims
    chan, ns, pix = sup_ref.shape
    nt = res_ref.shape[0]
    pool_rows = pool_ref.shape[0]
    classes = ridge_ref.shape[1]
    per_owner = res_ref.shape[1]
    qn = side // SUBL
    mtile = pix // SUBL
    stride_q = (side + 2) * SUBL
    me = lax.axis_index("sup")
    grp = lax.axis_index("tgt")
    half = nt // 2
    far_first = sorted(range(1, n_sup), key=lambda d: -min(d, n_sup - d))

    barrier = pltpu.get_barrier_semaphore()
    for d in range(1, n_sup):
        pl.semaphore_signal(barrier, inc=1, device_id=(grp, lax.rem(me + d, n_sup)), device_id_type=MESH)
    for d in range(1, n_tgt):
        pl.semaphore_signal(barrier, inc=1, device_id=(lax.rem(grp + d, n_tgt), me), device_id_type=MESH)

    base = (grp * n_sup + me) * pool_rows
    ids = idx_ref[...] - base
    row_id = lax.broadcasted_iota(jnp.int32, (pool_rows, n_tgt * nt), 0)
    selector = (row_id == ids).astype(F32).astype(BF16)
    for ch in range(n_chunk):
        block = dot0(selector, pool_ref[:, ch * width:(ch + 1) * width]).astype(BF16)
        for g in range(n_tgt):
            for h in range(2):
                psend[g, h * n_chunk + ch] = block[g * nt + h * half:g * nt + (h + 1) * half]
    pl.semaphore_wait(barrier, n_sup + n_tgt - 2)

    def class_tile(k):
        return pl.ds(pl.multiple_of(((k * per_owner) // LANES) * LANES, LANES), LANES)

    def ridge_copy(d):
        peer = lax.rem(me + d, n_sup)
        return pltpu.make_async_remote_copy(
            src_ref=ridge_ref.at[:, class_tile(peer)], dst_ref=rcls.at[me],
            send_sem=r_s.at[d - 1], recv_sem=r_r.at[d - 1],
            device_id=(grp, peer), device_id_type=MESH,
        )

    def tgt_copy(d):
        return pltpu.make_async_remote_copy(
            src_ref=psend.at[lax.rem(grp + d, n_tgt)], dst_ref=prec.at[d - 1],
            send_sem=p_s.at[d - 1], recv_sem=p_r.at[d - 1],
            device_id=(lax.rem(grp + d, n_tgt), me), device_id_type=MESH,
        )

    for d in range(1, n_tgt):
        tgt_copy(d).start()
    for d in far_first:
        ridge_copy(d).start()
    rcls[me] = ridge_ref[:, class_tile(me)]
    for d in range(1, n_tgt):
        tgt_copy(d).wait_recv()
    total = psend[grp]
    for d in range(1, n_tgt):
        total = total + prec[d - 1]
    pown[...] = total

    def rs_copy(d):
        peer = lax.rem(me + d, n_sup)
        return peer, pltpu.make_async_remote_copy(
            src_ref=pown.at[lax.rem(peer, n_shards)], dst_ref=rsbuf.at[d - 1],
            send_sem=rs_s.at[d - 1], recv_sem=rs_r.at[d - 1],
            device_id=(grp, peer), device_id_type=MESH,
        )

    def when(cond, fn):
        if n_shards == n_sup:
            fn()
        else:
            pl.when(cond)(fn)

    for d in far_first:
        peer, copy = rs_copy(d)
        when(peer < n_shards, copy.start)

    for c in range(chan):
        s8[c, ns:, :] = jnp.zeros((SUBL - ns, pix), F32)
        s8[c, :ns, :] = sup_ref[c]
    sup_self = s8[0] * s8[0]
    for c in range(1, chan):
        sup_self = sup_self + s8[c] * s8[c]
    svs = self_vars(sup_self / chan, side)
    row8 = lax.broadcasted_iota(jnp.int32, (SUBL, LANES), 0)
    lane8 = lax.broadcasted_iota(jnp.int32, (SUBL, LANES), 1)
    hot_j = (row8 == lane8 // nt).astype(F32)
    for depth in range(LAYERS):
        svar[depth] = svs[depth]
    def stacked(x):
        return jnp.concatenate([y.astype(F32) for y in split3(x)], axis=0).astype(BF16)

    hot_j3 = jnp.concatenate([hot_j] * 3, axis=0).astype(BF16)
    for c in range(chan):
        parts = stacked(s8[c])
        for s in range(SUBL):
            cut = slice(s * mtile, (s + 1) * mtile)
            sexp[c, cut, :] = dot0(parts[:, cut], hot_j3)
    for depth in range(LAYERS):
        parts = stacked(lax.rsqrt(1.0 + 2.0 * svs[depth]))
        for s in range(SUBL):
            cut = slice(s * mtile, (s + 1) * mtile)
            rbexp[depth, cut, :] = dot0(parts[:, cut], hot_j3)
    zero_tile = jnp.zeros((SUBL, LANES), F32)
    for buf in (pad_a, pad_b):
        for q in range(qn):
            buf[q * stride_q:q * stride_q + SUBL, :] = zero_tile
            buf[(q + 1) * stride_q - SUBL:(q + 1) * stride_q, :] = zero_tile

    def ag_copy(d):
        return pltpu.make_async_remote_copy(
            src_ref=tbuf.at[lax.rem(me, n_shards)], dst_ref=tbuf.at[lax.rem(me, n_shards)],
            send_sem=ag_s.at[d - 1], recv_sem=ag_r.at[d - 1],
            device_id=(grp, lax.rem(me + d, n_sup)), device_id_type=MESH,
        )

    def own_shard():
        acc = pown[me].astype(F32)
        for d in range(1, n_sup):
            rs_copy(d)[1].wait_recv()
            acc = acc + rsbuf[d - 1].astype(F32)
        tbuf[me] = acc.astype(BF16)
        for d in far_first:
            ag_copy(d).start()

    when(me < n_shards, own_shard)

    first = me * per_owner
    chunk = (first // LANES) * LANES
    lane_c = lax.broadcasted_iota(jnp.int32, (ns, LANES), 1) + chunk
    own_class = (lane_c >= first) & (lane_c < first + per_owner)
    for d in range(1, n_sup):
        ridge_copy(d).wait_recv()
    for k in range(n_sup):
        rown[k, :ns, :] = jnp.where(own_class, rcls[k], 0.0)
        rown[k, ns:, :] = jnp.zeros((SUBL - ns, LANES), F32)
    rows = rown[...].reshape(n_sup * SUBL, LANES)
    psrc[...] = lax.dot_general(
        rows, rows, (((1,), (1,)), ((), ())), precision=HI, preferred_element_type=F32
    ).reshape(n_sup, SUBL, n_sup * SUBL)

    def gram_copy(d):
        peer = lax.rem(me + d, n_sup)
        return pltpu.make_async_remote_copy(
            src_ref=psrc.at[peer], dst_ref=pdst.at[d - 1],
            send_sem=q_s.at[d - 1], recv_sem=q_r.at[d - 1],
            device_id=(grp, peer), device_id_type=MESH,
        )

    for d in far_first:
        gram_copy(d).start()
    row_t = lax.broadcasted_iota(jnp.int32, (nt, LANES), 0)
    lane_t = lax.broadcasted_iota(jnp.int32, (nt, LANES), 1)
    hot_i = (row_t == lane_t % nt).astype(F32).astype(BF16)
    for d in range(1, n_sup):
        when(lax.rem(me - d + n_sup, n_sup) < n_shards, ag_copy(d).wait_recv)

    for h in range(2):
        for ch in range(n_chunk):
            tfull[h * half:(h + 1) * half, ch * width:(ch + 1) * width] = tbuf[h * n_chunk + ch]

    tgt_self = jnp.zeros((nt, pix), F32)
    for c in range(chan):
        t = tfull[:, c * pix:(c + 1) * pix].astype(F32)
        tgt_self = tgt_self + t * t
    tvs = self_vars(tgt_self / chan, side)
    hot_i3 = jnp.concatenate([hot_i] * 3, axis=0)
    for s in range(SUBL):
        cut = slice(s * mtile, (s + 1) * mtile)
        pair0 = jnp.zeros((mtile, LANES), F32)
        for c in range(chan):
            t = dot0(tfull[:, c * pix + s * mtile:c * pix + (s + 1) * mtile], hot_i)
            texp[c, pl.ds(s, mtile, stride=SUBL), :] = t
            pair0 = pair0 + t * sexp[c, cut, :]
        pair0 = pair0 / chan
        for q in range(qn):
            pad_a[pl.ds(q * stride_q + SUBL + s, side, stride=SUBL), :] = pair0[q * side:(q + 1) * side]
        for depth in range(LAYERS):
            inv = lax.rsqrt(1.0 + 2.0 * tvs[depth][:, cut])
            wide = dot0(jnp.concatenate(split3(inv), axis=0), hot_i3)
            wbuf[depth, pl.ds(s, mtile, stride=SUBL), :] = wide * rbexp[depth, cut, :]

    sub = lax.broadcasted_iota(jnp.int32, (SUBL, LANES), 0)

    def box_column(buf, c):
        sums = []
        for q in range(qn):
            def at(k):
                return buf[pl.ds(pl.multiple_of(q * stride_q + (c + k) * SUBL, SUBL), SUBL), :]
            sums.append(at(0) + at(1) + at(2))
        up = jnp.where(sub > 0, pltpu.roll(sums[-1], 1, 0), 0.0)
        down = jnp.where(sub < SUBL - 1, pltpu.roll(sums[0], SUBL - 1, 0), 0.0)
        ext = [up] + sums + [down]
        return [ext[q] + ext[q + 1] + ext[q + 2] for q in range(qn)]

    def tile(q, c):
        return pl.ds(pl.multiple_of((q * side + c) * SUBL, SUBL), SUBL)

    def padded(q, c):
        return pl.ds(pl.multiple_of(q * stride_q + (c + 1) * SUBL, SUBL), SUBL)

    def forward(depth, src, dst):
        def body(c, acc):
            sums = box_column(src, c)
            for q in range(qn):
                w = wbuf[depth, tile(q, c), :]
                ang = (sums[q] * (4.0 / 9.0) + 0.2) * w
                der = TWO_PI * lax.rsqrt(1.0 - ang * ang)
                a1[depth, tile(q, c), :] = der * w
                a2[depth, tile(q, c), :] = der * ang
                pair = TWO_PI * arcsin(ang)
                if dst is None:
                    acc = acc + pair
                else:
                    dst[padded(q, c), :] = pair
            return acc
        return lax.fori_loop(0, side, body, zero_tile, unroll=4)

    bufs = (pad_a, pad_b)
    for depth in range(LAYERS - 1):
        forward(depth, bufs[depth % 2], bufs[(depth + 1) % 2])
    acc = forward(LAYERS - 1, bufs[(LAYERS - 1) % 2], None)
    krow = jnp.sum(acc, axis=0, keepdims=True) / pix
    krows = jnp.broadcast_to(krow, (SUBL, LANES))
    turn = (row8 + SUBL * ns - lane8 // nt) % ns
    ktile = krows
    for d in range(1, ns):
        ktile = jnp.where(turn == d, pltpu.roll(krows, LANES - d * nt, 1), ktile)
    kbuf[me] = ktile

    def k_copy(d):
        return pltpu.make_async_remote_copy(
            src_ref=kbuf.at[me], dst_ref=kbuf.at[me],
            send_sem=k_s.at[d - 1], recv_sem=k_r.at[d - 1],
            device_id=(grp, lax.rem(me + d, n_sup)), device_id_type=MESH,
        )

    for d in far_first:
        k_copy(d).start()

    mine = jnp.concatenate([ridge_ref[...], jnp.zeros((SUBL - ns, classes), F32)], axis=0)
    labels = lab_ref[...].astype(F32)
    lab_row = jnp.dot(
        jnp.broadcast_to(labels, (SUBL, nt)), hot_i.astype(F32), precision=HI, preferred_element_type=F32
    )[0:1]
    class_id = lax.broadcasted_iota(jnp.int32, (classes, LANES), 0).astype(F32)
    label_hot = (class_id == lab_row).astype(F32).astype(BF16)
    picked = jnp.dot(stacked(mine), label_hot, preferred_element_type=F32)
    picked = picked[:SUBL] + picked[SUBL:2 * SUBL] + picked[2 * SUBL:]
    lab_term = jnp.sum(picked * hot_j, axis=0, keepdims=True)

    gram = psrc[me]
    for d in range(1, n_sup):
        gram_copy(d).wait_recv()
        gram = gram + pdst[d - 1]
    coef[...] = dot0(gram, hot_j, HI)

    for d in range(1, n_sup):
        k_copy(d).wait_recv()
    kall = kbuf[...].reshape(n_sup * SUBL, LANES)
    kg = jnp.sum(kall * coef[...], axis=0, keepdims=True) - lab_term
    scale = float(side * side) / nt / pix
    top = jnp.broadcast_to(kg * scale, (SUBL, LANES))

    def backward(depth, src, dst):
        def body(c, carry):
            if src is None:
                grads = [top] * qn
            else:
                grads = [x * (4.0 / 9.0) for x in box_column(src, c)]
            for q in range(qn):
                dst[padded(q, c), :] = grads[q] * a1[depth, tile(q, c), :]
                hs[depth, tile(q, c), :] = grads[q] * a2[depth, tile(q, c), :]
            return carry
        lax.fori_loop(0, side, body, 0, unroll=4)

    src = None
    for step, depth in enumerate(reversed(range(LAYERS))):
        backward(depth, src, bufs[step % 2])
        src = bufs[step % 2]

    def input_grad(c, carry):
        grads = [x * (4.0 / 9.0 / chan) for x in box_column(src, c)]
        for q in range(qn):
            for ch in range(chan):
                hs[LAYERS + ch, tile(q, c), :] = grads[q] * texp[ch, tile(q, c), :]
        return carry
    lax.fori_loop(0, side, input_grad, 0, unroll=4)

    row_l = lax.broadcasted_iota(jnp.int32, (LANES, LANES), 0)
    col_l = lax.broadcasted_iota(jnp.int32, (LANES, LANES), 1)
    gather = [
        (col_l == a * SUBL + row_l // nt).astype(F32).astype(BF16) for a in range(LAYERS + chan)
    ]
    gather = [jnp.concatenate([x, x], axis=0) for x in gather]
    blk = 256
    for b in range(pix // blk):
        total = jnp.zeros((blk, LANES), F32)
        for a in range(LAYERS + chan):
            x = hs[a, b * blk:(b + 1) * blk, :]
            hi = x.astype(BF16)
            low = (x - hi.astype(F32)).astype(BF16)
            total = total + jnp.dot(
                jnp.concatenate([hi, low], axis=1), gather[a], preferred_element_type=F32
            )
        usum[b * blk:(b + 1) * blk, :] = total
    for s in range(SUBL):
        turned = usum[pl.ds(s, mtile, stride=SUBL), :].T
        ut[:, s * mtile:(s + 1) * mtile] = turned[:(LAYERS + chan) * SUBL]

    dact = None
    for depth in reversed(range(LAYERS)):
        var = svar[depth]
        dvar = -ut[depth * SUBL:(depth + 1) * SUBL, :] / (1.0 + 2.0 * var)
        if dact is not None:
            dvar = dvar + dact * (2.0 * TWO_PI) * lax.rsqrt(1.0 + 4.0 * var) / (1.0 + 2.0 * var)
        dact = (2.0 / 9.0) * box_rows(dvar, side)
    for c in range(chan):
        a = LAYERS + c
        gsend[c] = ut[a * SUBL:(a + 1) * SUBL, :] + dact * (2.0 / chan) * s8[c]

    def g_copy(d):
        return pltpu.make_async_remote_copy(
            src_ref=gsend, dst_ref=grecv.at[d - 1],
            send_sem=g_s.at[d - 1], recv_sem=g_r.at[d - 1],
            device_id=(lax.rem(grp + d, n_tgt), me), device_id_type=MESH,
        )

    for d in range(1, n_tgt):
        g_copy(d).start()

    pred = dot0(kall[:, :nt], rows, HI)
    lab_col = jnp.sum(jnp.where(row_t == lane_t, lab_row, 0.0), axis=1, keepdims=True)
    pred = pred - ((lane_t + chunk).astype(F32) == lab_col).astype(F32)
    pred = pltpu.roll(pred, lax.rem(LANES - first % LANES, LANES), 1)
    res_ref[...] = pred[:, :per_owner]

    for d in range(1, n_tgt):
        g_copy(d).wait_recv()
    for c in range(chan):
        terms = gsend[c]
        if n_tgt == 2:
            terms = terms + grecv[0, c]
        else:
            terms = jnp.zeros_like(terms)
            for g in range(n_tgt):
                dist = lax.rem(grp - g + n_tgt, n_tgt)
                part = grecv[jnp.maximum(dist - 1, 0), c]
                terms = terms + jnp.where(dist == 0, gsend[c], part)
        grad_ref[c] = terms[:ns]

    for d in range(1, n_tgt):
        tgt_copy(d).wait_send()
        g_copy(d).wait_send()
    for d in range(1, n_sup):
        peer, copy = rs_copy(d)
        when(peer < n_shards, copy.wait_send)
        when(me < n_shards, ag_copy(d).wait_send)
        ridge_copy(d).wait_send()
        gram_copy(d).wait_send()
        k_copy(d).wait_send()


def solution(mesh):
    n_tgt, n_sup = mesh.shape["tgt"], mesh.shape["sup"]

    def local(image_pool, target_index, labels, support, ridge_coef):
        nt = labels.shape[0]
        ns, chan, pix = support.shape
        side = math.isqrt(pix)
        classes = ridge_coef.shape[1]
        per_owner = classes // n_sup
        lane_tiles = chan * pix // LANES
        n_chunk = max(k for k in range(1, lane_tiles + 1) if lane_tiles % k == 0 and 2 * k <= n_sup)
        n_shards = 2 * n_chunk
        width = chan * pix // n_chunk
        dims = (n_tgt, n_sup, n_shards, n_chunk, width, side)
        half = nt // 2
        pad_rows = (side // SUBL) * (side + 2) * SUBL
        shard = (n_shards, half, width)
        dma = pltpu.SemaphoreType.DMA
        sems = []
        for n in (n_tgt, n_sup, n_sup, n_sup, n_sup, n_sup, n_tgt):
            sems += [dma((n - 1,)), dma((n - 1,))]
        f32map = lambda n: pltpu.VMEM((n, pix, LANES), F32)
        scratch = [
            pltpu.VMEM((n_tgt,) + shard, BF16),
            pltpu.VMEM(shard, BF16),
            pltpu.VMEM((n_tgt - 1,) + shard, BF16),
            pltpu.VMEM((n_sup - 1, half, width), BF16),
            pltpu.VMEM(shard, BF16),
            pltpu.VMEM((nt, chan * pix), BF16),
            pltpu.VMEM((n_sup, ns, LANES), F32),
            pltpu.VMEM((n_sup, SUBL, LANES), F32),
            pltpu.VMEM((n_sup, SUBL, n_sup * SUBL), F32),
            pltpu.VMEM((n_sup - 1, SUBL, n_sup * SUBL), F32),
            pltpu.VMEM((n_sup, SUBL, LANES), F32),
            pltpu.VMEM((chan, SUBL, pix), F32),
            pltpu.VMEM((n_tgt - 1, chan, SUBL, pix), F32),
            pltpu.VMEM((chan, SUBL, pix), F32),
            f32map(chan),
            f32map(LAYERS),
            pltpu.VMEM((LAYERS, SUBL, pix), F32),
            f32map(chan),
            f32map(LAYERS),
            f32map(LAYERS),
            f32map(LAYERS),
            f32map(LAYERS + chan),
            pltpu.VMEM((pad_rows, LANES), F32),
            pltpu.VMEM((pad_rows, LANES), F32),
            pltpu.VMEM((pix, LANES), F32),
            pltpu.VMEM(((LAYERS + chan) * SUBL, pix), F32),
            pltpu.VMEM((n_sup * SUBL, LANES), F32),
        ] + sems
        vmem = pl.BlockSpec(memory_space=pltpu.VMEM)
        residual, grad = pl.pallas_call(
            functools.partial(kernel, dims),
            out_shape=(
                jax.ShapeDtypeStruct((nt, per_owner), F32),
                jax.ShapeDtypeStruct((chan, ns, pix), F32),
            ),
            in_specs=[vmem] * 5,
            out_specs=(vmem, vmem),
            scratch_shapes=scratch,
            compiler_params=pltpu.CompilerParams(collective_id=0, has_side_effects=True, vmem_limit_bytes=60000 * 1024),
        )(target_index.reshape(1, -1), labels.reshape(1, nt), image_pool, support.transpose(1, 0, 2), ridge_coef)
        return residual, grad.transpose(1, 0, 2)

    in_specs = (P(("tgt", "sup"), None), P(), P("tgt"), P("sup", None, None), P("sup", None))
    out_specs = (P("tgt", "sup"), P("sup", None, None))
    return jax.shard_map(local, mesh=mesh, in_specs=in_specs, out_specs=out_specs, check_vma=False)
```
